128 devices in a mesh: shell: 64 (over y, x, z), sky: 2 (over core).
Axes of the slice: x: 4, y: 4, z: 4, core: 2. Of those that a mesh axis runs over, the one named last changes fastest.
Arguments:
- excitation: float32 [2048, 65536], P('shell', 'sky'), may hold values from -1.8 to 1.8
- star_shell: int32 [128, 128, 128], P(('shell', 'sky')), may hold values from 0 to 31
- star_pixel: int32 [128, 128, 128], P(('shell', 'sky')), may hold values from 0 to 32767
- star_fraction: float32 [128, 128, 128], P(('shell', 'sky')), may hold values from 0 to 1
- star_count: int32 [128, 128], P(('shell', 'sky')), may hold values from 0 to 128, as said below
- observed: float32 [128, 128, 128], P(None, ('shell', 'sky')), may hold values from 0 to 1
- inverse_error: float32 [128, 128, 128], P(None, ('shell', 'sky')), may hold values from 1 to 8
Outputs:
- extinction: float32 [2048, 65536], P('shell', 'sky')
- sensitivity: float32 [2048, 65536], P('shell', 'sky')
- residual: float32 [128, 128, 128], P(None, ('shell', 'sky'))
The draws below stay inside these ranges and needn't reach their ends.
Inputs may be any that keep to these rules, and one draw needn't show every extreme that they name: `star_count`: live slots from holder h to owner o. In every draw some owner gets 128 live slots from every holder; holders' loads differ.
All inputs are finite; a program needn't handle non-finite values.
Results may differ from the reference program's by a relative error of at most 0.00018.
Values sent between devices are 32-bit elements; how exact they have to be, the bound alone decides.
No kernel may reach another device: no remote copies, remote signals or barrier semaphores. Data moves between devices by JAX's collectives and lax.ppermute only.
A program may use at most 128 MiB of HBM per device.

```python
import math
import jax
import jax.numpy as jnp

SHELL_DEV = 32
PIX_DEV = 32768
PASSES = 4
CAP = 128
SHELLS = 2048
PIXELS = 65536
HOLDERS = 128
N_SKY = 2


def draw_star_count(key, part):
    first_key, second_key, third_key = jax.random.split(jax.random.fold_in(key, 17), 3)
    uniform_part = jax.random.randint(first_key, (HOLDERS, HOLDERS), 0, CAP + 1)
    holder_level = jax.random.randint(second_key, (HOLDERS, 1), 2, 5)
    counted = jnp.minimum(uniform_part * holder_level // 2, CAP)
    full_owner = jax.random.randint(third_key, (), 0, HOLDERS)
    owner_index = jnp.arange(HOLDERS, dtype=jnp.int32)[None, :]
    return jnp.where(owner_index == full_owner, CAP, counted).astype(jnp.int32)


def touch_ends(array, rng, low, largest):
    index_at = [jax.random.randint(jax.random.fold_in(rng, axis), (), 0, length) for axis, length in enumerate(array.shape)]
    widest = array.shape.index(max(array.shape))
    neighbour = index_at[:widest] + [(index_at[widest] + 1) % array.shape[widest]] + index_at[widest + 1:]
    return array.at[tuple(index_at)].set(low).at[tuple(neighbour)].set(largest)


def levels(stream_key, dims, shards, smallest, top_value):
    loudness, own = 1.0, jax.random.fold_in(stream_key, 6)
    for dim, blocks in shards:
        draws = jnp.exp(jax.random.uniform(jax.random.fold_in(own, dim), (blocks,), jnp.float32, smallest / len(shards), top_value / len(shards)))
        loudness = loudness * jnp.repeat(draws, dims[dim] // blocks).reshape([-1 if axis == dim else 1 for axis in range(len(dims))])
    return loudness


def normal_values(own_key, extent, width, limit, shards=(), kind=jnp.bfloat16):
    array = width * jax.random.normal(own_key, extent, jnp.float32)
    if shards:
        array = array * levels(own_key, extent, shards, -0.22, 0.18)
    return jnp.clip(array, -limit, limit).astype(kind)


def setup_inputs(seed: int = 0) -> dict:
    seeds = jax.random.split(jax.random.key(seed), 8)
    excitation = normal_values(seeds[0], (SHELLS, PIXELS), 0.3, 1.8, ((0, 64), (1, 2)), jnp.float32)
    star_shell = touch_ends(jax.random.randint(seeds[1], (HOLDERS, HOLDERS, CAP), 0, SHELL_DEV), jax.random.fold_in(seeds[1], 1), 0, SHELL_DEV - 1).astype(jnp.int32)
    star_pixel = touch_ends(jax.random.randint(seeds[2], (HOLDERS, HOLDERS, CAP), 0, PIX_DEV), jax.random.fold_in(seeds[2], 1), 0, PIX_DEV - 1).astype(jnp.int32)
    star_fraction = jnp.clip(1.0 * jax.random.uniform(seeds[3], (HOLDERS, HOLDERS, CAP), jnp.float32) ** levels(seeds[3], (HOLDERS, HOLDERS, CAP), ((0, 128),), -0.2, 0.2), 0.0, 1.0)
    star_count = draw_star_count(jax.random.fold_in(seeds[7], 71), 0)
    observed = jnp.clip(1.0 * jax.random.uniform(seeds[5], (HOLDERS, HOLDERS, CAP), jnp.float32) ** levels(seeds[5], (HOLDERS, HOLDERS, CAP), ((1, 128),), -0.2, 0.2), 0.0, 1.0)
    inverse_error = jnp.clip(jnp.exp(math.log(8.0) - 2.0794415 * jax.random.uniform(seeds[6], (HOLDERS, HOLDERS, CAP), jnp.float32) ** levels(seeds[6], (HOLDERS, HOLDERS, CAP), ((1, 128),), -0.2, 0.2)), 1.0, 8.0)
    return {"excitation": excitation, "star_shell": star_shell, "star_pixel": star_pixel, "star_fraction": star_fraction, "star_count": star_count, "observed": observed, "inverse_error": inverse_error}


depth_span = 2.0


def reference(excitation, star_shell, star_pixel, star_fraction, star_count, observed, inverse_error):
    shells_all = excitation.shape[0]
    pixels_all = excitation.shape[1]
    thickness = depth_span / shells_all
    logdens = excitation
    for sweep in range(PASSES):
        padded = jnp.pad(logdens, ((1, 1), (0, 0)))
        logdens = 0.3 * (padded[:-2] + padded[2:]) + 0.35 * logdens + excitation
    density = jnp.exp(logdens)
    extinction = jnp.cumsum(density * thickness, axis=0)
    holder = jnp.arange(HOLDERS, dtype=jnp.int32)
    shell_index = (holder // N_SKY)[:, None, None] * SHELL_DEV + star_shell
    pixel_index = (holder % N_SKY)[:, None, None] * PIX_DEV + star_pixel
    slot_index = (shell_index * pixels_all + pixel_index).astype(jnp.int32)
    slot_alive = jnp.arange(CAP, dtype=jnp.int32)[None, None, :] < star_count[:, :, None]
    near_share = 1.0 - star_fraction
    looked = extinction.reshape(-1)[slot_index] - near_share * thickness * density.reshape(-1)[slot_index]
    column = jnp.where(slot_alive, looked, 0.0)
    transmit = jnp.exp(-column)
    residual = jnp.where(slot_alive, (observed - (1.0 - transmit)) * inverse_error, 0.0)
    pull_back = -residual * inverse_error * transmit
    flat_index = slot_index.reshape(-1)
    impulse = jnp.zeros((shells_all * pixels_all,), excitation.dtype)
    impulse = impulse.at[flat_index].add(pull_back.reshape(-1)).reshape(shells_all, pixels_all)
    nearby = jnp.zeros((shells_all * pixels_all,), excitation.dtype)
    nearby = nearby.at[flat_index].add((near_share * pull_back).reshape(-1)).reshape(shells_all, pixels_all)
    tail_sums = jnp.flip(jnp.cumsum(jnp.flip(impulse, 0), axis=0), 0)
    sensitivity = density * (tail_sums - nearby)
    return extinction, sensitivity, residual
```

```python
import jax
import jax.numpy as jnp
from jax import lax
from jax.experimental import pallas as pl
from jax.experimental.pallas import tpu as pltpu
from jax.sharding import PartitionSpec as P

PASSES = 4
LANES = 128
SUB = 8
SPARE = 8
ACCS = 4
BOTH = ("shell", "sky")


depth_span = 2.0


def cost(micros, nbytes):
    return pl.CostEstimate(flops=int(micros * 2e8), bytes_accessed=int(nbytes), transcendentals=0)


def density_kernel(shells, thickness, edge_ref, exc_ref, up_ref, down_ref, dens_ref, tab_ref, sum_ref):
    tall = shells + 1
    low_mask = edge_ref[0]
    high_mask = edge_ref[1]

    def group(g):
        exc = {}

        def load(r):
            if r < 0:
                return up_ref[pl.ds(g * SUB * PASSES + PASSES + r, SUB, stride=PASSES), :]
            if r >= shells:
                return down_ref[pl.ds(g * SUB * PASSES + r - shells, SUB, stride=PASSES), :]
            return exc_ref.at[r // SUB][pl.ds(g * SUB * SUB + r % SUB, SUB, stride=SUB), :]

        level = [dict() for _ in range(PASSES + 1)]
        tab_ref[pl.ds(g * SUB * tall, SUB, stride=tall), :] = jnp.zeros((SUB, LANES), jnp.float32)
        total = None
        for t in range(-PASSES, shells + PASSES):
            exc[t] = load(t)
            level[0][t] = exc[t]
            for k in range(1, PASSES + 1):
                r = t - k
                reach = PASSES - k
                if r < -reach or r >= shells + reach:
                    continue
                below = level[k - 1]
                value = 0.3 * (below[r - 1] + below[r + 1]) + 0.35 * below[r] + exc[r]
                if r < 0:
                    value = value * low_mask
                if r >= shells:
                    value = value * high_mask
                level[k][r] = value
            r = t - PASSES
            if r >= 0:
                dens = jnp.exp(level[PASSES][r])
                dens_ref[pl.ds((g * shells + r) * SUB, SUB), :] = dens
                step = dens * thickness
                total = step if total is None else total + step
                tab_ref[pl.ds(g * SUB * tall + 1 + r, SUB, stride=tall), :] = total
        sum_ref[pl.ds(g * SUB, SUB), :] = total

    for g in range(sum_ref.shape[0] // SUB):
        group(g)


def density_call(exc, up, down, edge, shells, groups, thickness):
    per = 32
    tall = shells + 1
    return pl.pallas_call(
        lambda *refs: density_kernel(shells, thickness, *refs),
        grid=(groups // per,),
        in_specs=[
            pl.BlockSpec(memory_space=pltpu.SMEM),
            pl.BlockSpec((shells // SUB, per * SUB, LANES), lambda i: (0, i, 0)),
            pl.BlockSpec((per * PASSES, LANES), lambda i: (i, 0)),
            pl.BlockSpec((per * PASSES, LANES), lambda i: (i, 0)),
        ],
        out_specs=[
            pl.BlockSpec((per * shells, LANES), lambda i: (i, 0)),
            pl.BlockSpec((per * tall, LANES), lambda i: (i, 0)),
            pl.BlockSpec((per, LANES), lambda i: (i, 0)),
        ],
        out_shape=[
            jax.ShapeDtypeStruct((groups * shells, LANES), jnp.float32),
            jax.ShapeDtypeStruct((groups * tall + SPARE, LANES), jnp.float32),
            jax.ShapeDtypeStruct((groups, LANES), jnp.float32),
        ],
        cost_estimate=cost(8, 12 << 20),
        name="density",
    )(edge, exc, up, down)


def lookup_kernel(first, idx_ref, tab_ref, frac_ref, out_ref):
    lane = lax.broadcasted_iota(jnp.int32, (SUB, LANES), 1)

    def body(o, carry):
        acc = [jnp.zeros((SUB, LANES), jnp.float32) for _ in range(4)]
        for c in range(LANES):
            packed = idx_ref[o + first, c]
            row = lax.shift_right_logical(packed, 7)
            value = pltpu.roll(tab_ref[pl.ds(row, SUB), :], packed & 127, 1)
            acc[c % 4] = jnp.where(lane == c, value, acc[c % 4])
        got = (acc[0] + acc[1]) + (acc[2] + acc[3])
        inner, outer = got[0:1], got[1:2]
        out_ref[pl.ds(o, 1), :] = inner + frac_ref[pl.ds(o + first, 1), :] * (outer - inner)
        return carry

    lax.fori_loop(0, out_ref.shape[0], body, 0)


def lookup_call(idx, tab, frac, first, count):
    return pl.pallas_call(
        lambda *refs: lookup_kernel(first, *refs),
        out_shape=jax.ShapeDtypeStruct((count, LANES), jnp.float32),
        in_specs=[
            pl.BlockSpec(memory_space=pltpu.SMEM),
            pl.BlockSpec(memory_space=pltpu.VMEM),
            pl.BlockSpec(memory_space=pltpu.VMEM),
        ],
        out_specs=pl.BlockSpec(memory_space=pltpu.VMEM),
        cost_estimate=cost(17, 5 << 20),
        name="lookup",
    )(idx, tab, frac)


def scan_kernel(reverse, in_ref, out_ref):
    n = in_ref.shape[0]
    order = range(n - 1, -1, -1) if reverse else range(n)
    total = jnp.zeros(in_ref.shape[1:], jnp.float32)
    for i in order:
        out_ref[i] = total
        total = total + in_ref[i]


def scan_call(parts, reverse):
    return pl.pallas_call(
        lambda *refs: scan_kernel(reverse, *refs),
        out_shape=jax.ShapeDtypeStruct(parts.shape, jnp.float32),
        cost_estimate=cost(1, 1 << 18),
        name="scan",
    )(parts)


def exclusive_sums(block, reverse):
    devices = lax.axis_size("shell")
    parts = block.reshape(devices, block.shape[0] // devices, LANES)
    parts = lax.all_to_all(parts, "shell", split_axis=0, concat_axis=0, tiled=True)
    parts = scan_call(parts, reverse)
    parts = lax.all_to_all(parts, "shell", split_axis=0, concat_axis=0, tiled=True)
    return parts.reshape(block.shape)


def halves(x):
    high = x.astype(jnp.bfloat16)
    return high, (x - high.astype(jnp.float32)).astype(jnp.bfloat16)


def star_kernel(pix_ref, off_ref, col_a_ref, col_b_ref, frac_ref, alive_ref, obs_ref, inv_ref,
                res_ref, here_ref, inner_ref, tail_ref, acc_ref):
    groups = off_ref.shape[0]
    rows = SUB
    offt = jnp.transpose(off_ref[...])
    offt = jnp.concatenate(halves(offt), axis=0)
    group_id = lax.broadcasted_iota(jnp.int32, (groups, LANES), 0)
    lane_id = lax.broadcasted_iota(jnp.int32, (LANES, LANES), 0)
    acc_ref[...] = jnp.zeros_like(acc_ref)

    def body(b, col_ref, shift):
        at = pl.ds(pl.multiple_of(b * rows, rows), rows)
        local = pl.ds(pl.multiple_of((b - shift) * rows, rows), rows)
        pix = pix_ref[at, :]
        high = lax.shift_right_logical(pix, 7)
        low = pix & 127
        pick = jnp.concatenate(
            [jnp.where(group_id == high[j:j + 1, :], 1.0, 0.0).astype(jnp.bfloat16) for j in range(rows)], axis=1)
        found = jnp.dot(offt, pick, preferred_element_type=jnp.float32)
        lanes = [lane_id == low[j:j + 1, :] for j in range(rows)]
        off_at = []
        for j in range(rows):
            part = found[:, j * LANES:(j + 1) * LANES]
            part = jnp.where(lanes[j], part[:LANES] + part[LANES:], 0.0)
            off_at.append(jnp.sum(part, axis=0, keepdims=True))
        column = col_ref[local, :] + jnp.concatenate(off_at, axis=0)
        transmit = jnp.exp(-column)
        inv = inv_ref[at, :]
        residual = jnp.where(alive_ref[at, :] > 0.0, (obs_ref[at, :] - (1.0 - transmit)) * inv, 0.0)
        pull = -residual * inv * transmit
        inner = (1.0 - frac_ref[at, :]) * pull
        res_ref[at, :] = residual
        here_ref[at, :] = pull - inner
        inner_ref[at, :] = inner
        spread = []
        for j in range(rows):
            spread.append(jnp.concatenate(halves(jnp.where(lanes[j], pull[j:j + 1, :], 0.0)), axis=0))
        spread = jnp.concatenate(spread, axis=1)
        acc_ref[...] += lax.dot_general(
            pick, spread, (((1,), (1,)), ((), ())), preferred_element_type=jnp.float32)

    half = col_a_ref.shape[0] // rows
    full = pix_ref.shape[0] // rows

    @pl.loop(0, half)
    def _(b):
        body(b, col_a_ref, 0)

    @pl.loop(half, full)
    def _(b):
        body(b, col_b_ref, half)

    tail_ref[...] = acc_ref[:, :LANES] + acc_ref[:, LANES:]


def star_call(pix, off, col_a, col_b, frac, alive, obs, inv):
    slots = jax.ShapeDtypeStruct(pix.shape, jnp.float32)
    return pl.pallas_call(
        star_kernel,
        out_shape=[slots, slots, slots, jax.ShapeDtypeStruct(off.shape, jnp.float32)],
        scratch_shapes=[pltpu.VMEM((off.shape[0], 2 * LANES), jnp.float32)],
        cost_estimate=cost(8, 1 << 20),
        name="star",
    )(pix, off, col_a, col_b, frac, alive, obs, inv)


def spread_kernel(first, count, start, idx_ref, here_ref, inner_ref, *refs):
    if start:
        start_ref, out_ref = refs[0], refs[1]
        accs = refs[2:]
    else:
        out_ref = refs[0]
        accs = refs[1:]
    total_rows = out_ref.shape[0]
    chunk = 64
    chunks = total_rows // chunk
    rest = total_rows - chunks * chunk

    def over(fn):
        def step(i, carry):
            fn(pl.ds(pl.multiple_of(i * chunk, chunk), chunk), chunk)
            return carry
        lax.fori_loop(0, chunks, step, 0)
        if rest:
            fn(pl.ds(chunks * chunk, rest), rest)

    def clear(rows, n):
        for k, acc in enumerate(accs):
            acc[rows, :] = start_ref[rows, :] if start and k == 0 else jnp.zeros((n, LANES), jnp.float32)

    over(clear)
    lane = lax.broadcasted_iota(jnp.int32, (SUB, LANES), 1)
    sub = lax.broadcasted_iota(jnp.int32, (SUB, LANES), 0)
    lane_a = jnp.where(sub == 0, lane, -1)
    lane_b = jnp.where(sub == 1, lane, -1)

    def body(o, carry):
        for c in range(LANES):
            packed = idx_ref[o, c]
            row = lax.shift_right_logical(packed, 7)
            low = packed & 127
            value = jnp.where(lane_a == low, inner_ref[o, c], jnp.where(lane_b == low, here_ref[o, c], 0.0))
            acc = accs[c % ACCS]
            acc[pl.ds(row, SUB), :] = acc[pl.ds(row, SUB), :] + value
        return carry

    lax.fori_loop(first, first + count, body, 0)

    def gather(rows, n):
        total = accs[0][rows, :]
        for acc in accs[1:]:
            total = total + acc[rows, :]
        out_ref[rows, :] = total

    over(gather)


def spread_call(idx, here, inner, rows, first, count, start=None):
    shape = (rows, LANES)
    extra = () if start is None else (start,)
    return pl.pallas_call(
        lambda *refs: spread_kernel(first, count, start is not None, *refs),
        out_shape=jax.ShapeDtypeStruct(shape, jnp.float32),
        in_specs=[pl.BlockSpec(memory_space=pltpu.SMEM)] * 3
        + [pl.BlockSpec(memory_space=pltpu.VMEM)] * len(extra),
        out_specs=pl.BlockSpec(memory_space=pltpu.VMEM),
        scratch_shapes=[pltpu.VMEM(shape, jnp.float32)] * ACCS,
        cost_estimate=cost(20, 5 << 20),
        name="spread",
    )(idx, here, inner, *extra)


def extinction_kernel(shells, tab_ref, off_ref, out_ref):
    tall = shells + 1
    for g in range(off_ref.shape[0] // SUB):
        off = off_ref[pl.ds(g * SUB, SUB), :]
        for r in range(shells):
            value = tab_ref[pl.ds(g * SUB * tall + 1 + r, SUB, stride=tall), :] + off
            out_ref.at[r // SUB][pl.ds(g * SUB * SUB + r % SUB, SUB, stride=SUB), :] = value


def extinction_call(tab, off, shells):
    groups = off.shape[0]
    per = 32
    return pl.pallas_call(
        lambda *refs: extinction_kernel(shells, *refs),
        grid=(groups // per,),
        in_specs=[
            pl.BlockSpec((per * (shells + 1), LANES), lambda i: (i, 0)),
            pl.BlockSpec((per, LANES), lambda i: (i, 0)),
        ],
        out_specs=pl.BlockSpec((shells // SUB, per * SUB, LANES), lambda i: (0, i, 0)),
        out_shape=jax.ShapeDtypeStruct((shells // SUB, groups * SUB, LANES), jnp.float32),
        cost_estimate=cost(4, 8 << 20),
        name="extinction",
    )(tab, off)


def sensitivity_kernel(shells, dens_ref, drop_ref, off_ref, out_ref):
    tall = shells + 1
    for g in range(off_ref.shape[0] // SUB):
        total = off_ref[pl.ds(g * SUB, SUB), :]
        for r in range(shells - 1, -1, -1):
            total = total + drop_ref[pl.ds(g * SUB * tall + 1 + r, SUB, stride=tall), :]
            out_ref.at[r // SUB][pl.ds(g * SUB * SUB + r % SUB, SUB, stride=SUB), :] = (
                dens_ref[pl.ds((g * shells + r) * SUB, SUB), :] * total)


def sensitivity_call(dens, drop, off, shells):
    groups = off.shape[0]
    per = 32
    return pl.pallas_call(
        lambda *refs: sensitivity_kernel(shells, *refs),
        grid=(groups // per,),
        in_specs=[
            pl.BlockSpec((per * shells, LANES), lambda i: (i, 0)),
            pl.BlockSpec((per * (shells + 1), LANES), lambda i: (i, 0)),
            pl.BlockSpec((per, LANES), lambda i: (i, 0)),
        ],
        out_specs=pl.BlockSpec((shells // SUB, per * SUB, LANES), lambda i: (0, i, 0)),
        out_shape=jax.ShapeDtypeStruct((shells // SUB, groups * SUB, LANES), jnp.float32),
        cost_estimate=cost(5, 12 << 20),
        name="sensitivity",
    )(dens, drop, off)


def to_tiles(x):
    shells, pixels = x.shape
    groups = pixels // LANES
    x = x.reshape(shells // SUB, SUB, groups, LANES).transpose(0, 2, 1, 3)
    return x.reshape(shells // SUB, groups * SUB, LANES)


def from_tiles(x):
    bands, rows, lanes = x.shape
    groups = rows // SUB
    x = x.reshape(bands, groups, SUB, lanes).transpose(0, 2, 1, 3)
    return x.reshape(bands * SUB, groups * lanes)


def edge_rows(x, rows):
    count, pixels = rows.stop - rows.start, x.shape[1]
    part = x[rows].reshape(count, pixels // LANES, LANES).transpose(1, 0, 2)
    return part


def body(excitation, star_shell, star_pixel, star_fraction, star_count, observed, inverse_error):
    shells, pixels = excitation.shape
    devices = lax.axis_size("shell")
    me = lax.axis_index("shell")
    thickness = depth_span / (shells * devices)
    groups = pixels // LANES
    tall = shells + 1
    owners = star_shell.shape[1]

    up = [(i, i + 1) for i in range(devices - 1)]
    down = [(i + 1, i) for i in range(devices - 1)]
    from_below = lax.ppermute(edge_rows(excitation, slice(shells - PASSES, shells)), "shell", up)
    from_above = lax.ppermute(edge_rows(excitation, slice(0, PASSES)), "shell", down)
    owned = jnp.stack((observed[:, 0], inverse_error[:, 0]), axis=1)
    held = lax.all_to_all(owned, BOTH, split_axis=0, concat_axis=0, tiled=True)

    shell, pixel, fraction = star_shell[0], star_pixel[0], star_fraction[0]
    slot = lax.broadcasted_iota(jnp.int32, shell.shape, 1)
    low = pixel & (LANES - 1)
    row = (pixel >> 7) * tall + shell
    look_idx = (row << 7) | ((slot - low) & (LANES - 1))
    add_idx = (row << 7) | low
    alive = (slot < star_count[0][:, None]).astype(jnp.float32)

    edge = jnp.stack(((me > 0).astype(jnp.float32), (me < devices - 1).astype(jnp.float32)))
    dens, tab, block_sum = density_call(
        to_tiles(excitation),
        from_below.reshape(groups * PASSES, LANES),
        from_above.reshape(groups * PASSES, LANES),
        edge, shells, groups, thickness)

    offset = exclusive_sums(block_sum, False)
    half = owners // 2
    col_a = lookup_call(look_idx, tab, fraction, 0, half)
    col_b = lookup_call(look_idx, tab, fraction, half, owners - half)

    residual, here, inner, tail = star_call(
        pixel, offset, col_a, col_b, fraction, alive, held[:, 0], held[:, 1])
    tail_offset = exclusive_sums(tail, True)
    residual = lax.all_to_all(residual[:, None, :], BOTH, split_axis=0, concat_axis=0, tiled=True)

    rows = groups * tall + SPARE
    drop = spread_call(add_idx, here, inner, rows, 0, half)
    drop = spread_call(add_idx, here, inner, rows, half, owners - half, drop)
    extinction = extinction_call(tab, offset, shells)
    sensitivity = sensitivity_call(dens, drop, tail_offset, shells)
    return from_tiles(extinction), from_tiles(sensitivity), residual


def solution(mesh):
    placed = (
        P("shell", "sky"),
        P(BOTH, None, None),
        P(BOTH, None, None),
        P(BOTH, None, None),
        P(BOTH, None),
        P(None, BOTH, None),
        P(None, BOTH, None),
    )
    return jax.shard_map(
        body,
        mesh=mesh,
        in_specs=placed,
        out_specs=(P("shell", "sky"), P("shell", "sky"), P(None, BOTH, None)),
        check_vma=False,
    )
```

```python
import jax
import jax.numpy as jnp
from jax import lax
from jax.experimental import pallas as pl
from jax.experimental.pallas import tpu as pltpu
from jax.sharding import PartitionSpec as P

PASSES = 4
LANES = 128
SUB = 8
LEAD = 8
ACCS = 4
CHUNKS = 8
SPLIT = 7
PACK = 64
FIELDS = 4
BOTH = ("shell", "sky")


depth_span = 2.0

VMEM = pl.BlockSpec(memory_space=pltpu.VMEM)
SMEM = pl.BlockSpec(memory_space=pltpu.SMEM)
ANY = pl.BlockSpec(memory_space=pl.ANY)


def cost(micros, nbytes):
    return pl.CostEstimate(flops=int(micros * 2e8), bytes_accessed=int(nbytes), transcendentals=0)


def taps():
    power = [1.0]
    total = [0.0] * (2 * PASSES + 1)
    for k in range(PASSES + 1):
        for i, v in enumerate(power):
            total[PASSES - k + i] += v
        wider = [0.0] * (len(power) + 2)
        for i, v in enumerate(power):
            wider[i] += 0.3 * v
            wider[i + 1] += 0.35 * v
            wider[i + 2] += 0.3 * v
        power = wider
    return total[PASSES:]


def table_rows(groups, tall):
    unit = SPLIT * PACK
    return -(-(LEAD + groups * tall + SUB) // unit) * unit


def density_kernel(shells, groups, devices, thickness, edge_ref, obs_ref, inv_ref, exc_hbm, up_hbm, down_hbm,
                   dens_hbm, tab_hbm, pay_ref, exc_ref, up_ref, down_ref, dens_ref, tab_ref, in_sem, out_sem):
    tall = shells + 1
    per = groups // CHUNKS
    weight = taps()
    low_edge = edge_ref[0]
    high_edge = edge_ref[1]

    def inputs(i):
        wide = pl.ds(i * per * SUB, per * SUB)
        thin = pl.ds(i * per * PASSES, per * PASSES)
        return [
            pltpu.make_async_copy(exc_hbm.at[:, wide, :], exc_ref.at[:, wide, :], in_sem.at[0, i]),
            pltpu.make_async_copy(up_hbm.at[thin, :], up_ref.at[thin, :], in_sem.at[1, i]),
            pltpu.make_async_copy(down_hbm.at[thin, :], down_ref.at[thin, :], in_sem.at[2, i]),
        ]

    def outputs(i):
        flat = pl.ds(i * per * shells, per * shells)
        tall_rows = pl.ds(LEAD + i * per * tall, per * tall)
        return [
            pltpu.make_async_copy(dens_ref.at[flat, :], dens_hbm.at[flat, :], out_sem.at[0, i]),
            pltpu.make_async_copy(tab_ref.at[tall_rows, :], tab_hbm.at[tall_rows, :], out_sem.at[1, i]),
        ]

    for i in range(CHUNKS):
        for copy in inputs(i):
            copy.start()
    pay_ref[pl.ds(0, devices, stride=FIELDS), :] = obs_ref[...]
    pay_ref[pl.ds(1, devices, stride=FIELDS), :] = inv_ref[...]

    def group(g):
        exc = {}
        for r in range(shells):
            exc[r] = exc_ref.at[r // SUB][pl.ds(g * SUB * SUB + r % SUB, SUB, stride=SUB), :]
        for k in range(PASSES):
            low = up_ref[pl.ds(g * SUB * PASSES + PASSES - 1 - k, SUB, stride=PASSES), :]
            high = down_ref[pl.ds(g * SUB * PASSES + k, SUB, stride=PASSES), :]
            if k:
                low = low - low_edge * exc[k - 1]
                high = high - high_edge * exc[shells - k]
            exc[-1 - k] = low
            exc[shells + k] = high
        tab_ref[pl.ds(LEAD + g * SUB * tall, SUB, stride=tall), :] = jnp.zeros((SUB, LANES), jnp.float32)
        total = None
        for r in range(shells):
            value = weight[0] * exc[r]
            for k in range(1, PASSES + 1):
                value = value + weight[k] * (exc[r - k] + exc[r + k])
            dens = jnp.exp(value)
            dens_ref[pl.ds((g * shells + r) * SUB, SUB), :] = dens
            step = dens * thickness
            total = step if total is None else total + step
            tab_ref[pl.ds(LEAD + g * SUB * tall + 1 + r, SUB, stride=tall), :] = total
        first = g * SUB
        pay_ref[pl.ds((first % devices) * FIELDS + 2 + first // devices, SUB, stride=FIELDS), :] = total

    def chunk(i, carry):
        for copy in inputs(i):
            copy.wait()
        for k in range(per // SUB):
            group(i * (per // SUB) + k)
        for copy in outputs(i):
            copy.start()
        return carry

    lax.fori_loop(0, CHUNKS, chunk, 0)
    for i in range(CHUNKS):
        for copy in outputs(i):
            copy.wait()


def density_call(exc, up, down, edge, obs, inv, shells, groups, devices, thickness):
    tall = shells + 1
    rows = table_rows(groups, tall)
    return pl.pallas_call(
        lambda *refs: density_kernel(shells, groups, devices, thickness, *refs),
        in_specs=[SMEM, VMEM, VMEM, ANY, ANY, ANY],
        out_specs=[ANY, ANY, VMEM],
        out_shape=[
            jax.ShapeDtypeStruct((groups * shells, LANES), jnp.float32),
            jax.ShapeDtypeStruct((rows, LANES), jnp.float32),
            jax.ShapeDtypeStruct((devices * FIELDS, LANES), jnp.float32),
        ],
        scratch_shapes=[
            pltpu.VMEM(exc.shape, jnp.float32),
            pltpu.VMEM(up.shape, jnp.float32),
            pltpu.VMEM(down.shape, jnp.float32),
            pltpu.VMEM((groups * shells, LANES), jnp.float32),
            pltpu.VMEM((rows, LANES), jnp.float32),
            pltpu.SemaphoreType.DMA((3, CHUNKS)),
            pltpu.SemaphoreType.DMA((2, CHUNKS)),
        ],
        cost_estimate=cost(8, 12 << 20),
        name="density",
    )(edge, obs, inv, exc, up, down)


def lookup_kernel(first, idx_ref, tab_ref, low_ref, frac_ref, out_ref):
    lane = lax.broadcasted_iota(jnp.int32, (SUB, LANES), 1)
    sub = lax.broadcasted_iota(jnp.int32, (SUB, LANES), 0)
    pair = [(sub >> 1) == j for j in range(4)]
    quad = lane >> 2
    is_inner = sub == (lane & 3) * 2
    is_outer = sub == (lane & 3) * 2 + 1

    def body(o, carry):
        low = jnp.broadcast_to(low_ref[pl.ds(o + first, 1), :], (SUB, LANES))
        got = jnp.zeros((SUB, LANES), jnp.float32)
        for k in range(LANES // 4):
            rows = tab_ref[pl.ds(idx_ref[o + first, 4 * k], SUB), :]
            for j in range(1, 4):
                rows = jnp.where(pair[j], tab_ref[pl.ds(idx_ref[o + first, 4 * k + j] - 2 * j, SUB), :], rows)
            got = jnp.where(quad == k, jnp.take_along_axis(rows, low, axis=1), got)
        inner = jnp.sum(jnp.where(is_inner, got, 0.0), axis=0, keepdims=True)
        outer = jnp.sum(jnp.where(is_outer, got, 0.0), axis=0, keepdims=True)
        out_ref[pl.ds(o, 1), :] = inner + frac_ref[pl.ds(o + first, 1), :] * (outer - inner)
        return carry

    lax.fori_loop(0, out_ref.shape[0], body, 0)


def lookup_call(idx, tab, low, frac, first, count):
    return pl.pallas_call(
        lambda *refs: lookup_kernel(first, *refs),
        out_shape=jax.ShapeDtypeStruct((count, LANES), jnp.float32),
        in_specs=[SMEM, VMEM, VMEM, VMEM],
        out_specs=VMEM,
        cost_estimate=cost(15, 5 << 20),
        name="lookup",
    )(idx, tab, low, frac)


def scan_kernel(reverse, in_ref, out_ref, *field_ref):
    blocks = in_ref.shape[0] // SUB
    total = jnp.zeros((SUB, LANES), jnp.float32)
    for b in range(blocks - 1, -1, -1) if reverse else range(blocks):
        out_ref[4 * b:4 * b + 2, :] = total[2:4]
        out_ref[4 * b + 2:4 * b + 4, :] = total[6:8]
        total = total + in_ref[SUB * b:SUB * (b + 1), :]
    if field_ref:
        field_ref[0][...] = in_ref[pl.ds(0, field_ref[0].shape[0], stride=FIELDS), :]


def scan_call(parts, devices, reverse, field):
    shapes = [jax.ShapeDtypeStruct((devices * (FIELDS - 2), LANES), jnp.float32)]
    if field:
        shapes.append(jax.ShapeDtypeStruct((devices, LANES), jnp.float32))
    return pl.pallas_call(
        lambda *refs: scan_kernel(reverse, *refs),
        out_shape=shapes,
        cost_estimate=cost(1, 1 << 18),
        name="scan",
    )(parts)


def exchange(rows, devices):
    parts = rows.reshape(devices, rows.shape[0] // devices, LANES)
    parts = lax.all_to_all(parts, BOTH, split_axis=0, concat_axis=0, tiled=True)
    return parts.reshape(rows.shape)


def halves(x):
    high = x.astype(jnp.bfloat16)
    return high, (x - high.astype(jnp.float32)).astype(jnp.bfloat16)


def star_kernel(devices, count_ref, pix_ref, off_ref, held_ref, col_a_ref, col_b_ref, frac_ref,
                pay_ref, here_ref, inner_ref, acc_ref, tail_ref):
    groups = off_ref.shape[0]
    rows = SUB
    offt = jnp.transpose(off_ref[...])
    offt = jnp.concatenate(halves(offt), axis=0)
    group_id = lax.broadcasted_iota(jnp.int32, (groups, LANES), 0).astype(jnp.bfloat16)
    lane_id = lax.broadcasted_iota(jnp.int32, (LANES, LANES), 0)
    slot = lax.broadcasted_iota(jnp.int32, (rows, LANES), 1)
    sub = lax.broadcasted_iota(jnp.int32, (rows, LANES), 0)
    one = jnp.ones((groups, LANES), jnp.bfloat16)
    zero = jnp.zeros((groups, LANES), jnp.bfloat16)
    acc_ref[...] = jnp.zeros_like(acc_ref)
    pay_ref[pl.ds(1, devices, stride=FIELDS), :] = jnp.zeros((devices, LANES), jnp.float32)

    def body(b, col_ref, shift):
        at = pl.ds(pl.multiple_of(b * rows, rows), rows)
        local = pl.ds(pl.multiple_of((b - shift) * rows, rows), rows)
        pix = pix_ref[at, :]
        high = lax.shift_right_logical(pix, 7)
        high = (lax.rem(high, devices)) * (groups // devices) + lax.div(high, devices)
        high = high.astype(jnp.float32).astype(jnp.bfloat16)
        low = pix & 127
        pick = jnp.concatenate([jnp.where(group_id == high[j:j + 1, :], one, zero) for j in range(rows)], axis=1)
        found = jnp.dot(offt, pick, preferred_element_type=jnp.float32)
        lanes = [lane_id == low[j:j + 1, :] for j in range(rows)]
        off_at = []
        for j in range(rows):
            part = found[:, j * LANES:(j + 1) * LANES]
            part = jnp.where(lanes[j], part[:LANES] + part[LANES:], 0.0)
            off_at.append(jnp.sum(part, axis=0, keepdims=True))
        column = col_ref[local, :] + jnp.concatenate(off_at, axis=0)
        transmit = jnp.exp(-column)
        obs = held_ref[pl.ds(b * rows * FIELDS, rows, stride=FIELDS), :]
        inv = held_ref[pl.ds(b * rows * FIELDS + 1, rows, stride=FIELDS), :]
        live = jnp.zeros((rows, LANES), jnp.int32)
        for j in range(rows):
            live = jnp.where(sub == j, count_ref[0, b * rows + j], live)
        residual = jnp.where(slot < live, (obs - (1.0 - transmit)) * inv, 0.0)
        pull = -residual * inv * transmit
        inner = (1.0 - frac_ref[at, :]) * pull
        pay_ref[pl.ds(b * rows * FIELDS, rows, stride=FIELDS), :] = residual
        here_ref[at, :] = pull - inner
        inner_ref[at, :] = inner
        spread = []
        for j in range(rows):
            spread.append(jnp.concatenate(halves(jnp.where(lanes[j], pull[j:j + 1, :], 0.0)), axis=0))
        spread = jnp.concatenate(spread, axis=1)
        acc_ref[...] += lax.dot_general(
            pick, spread, (((1,), (1,)), ((), ())), preferred_element_type=jnp.float32)

    half = col_a_ref.shape[0] // rows
    full = pix_ref.shape[0] // rows

    @pl.loop(0, half)
    def _(b):
        body(b, col_a_ref, 0)

    @pl.loop(half, full)
    def _(b):
        body(b, col_b_ref, half)

    tail_ref[...] = acc_ref[:, :LANES] + acc_ref[:, LANES:]
    for e in range(groups // devices):
        pay_ref[pl.ds(2 + e, devices, stride=FIELDS), :] = tail_ref[pl.ds(e, devices, stride=groups // devices), :]


def star_call(count, pix, off, held, col_a, col_b, frac, devices):
    slots = jax.ShapeDtypeStruct(pix.shape, jnp.float32)
    return pl.pallas_call(
        lambda *refs: star_kernel(devices, *refs),
        out_shape=[jax.ShapeDtypeStruct(held.shape, jnp.float32), slots, slots],
        in_specs=[SMEM] + [VMEM] * 6,
        out_specs=[VMEM] * 3,
        scratch_shapes=[pltpu.VMEM((off.shape[0], 2 * LANES), jnp.float32), pltpu.VMEM(off.shape, jnp.float32)],
        cost_estimate=cost(8, 1 << 20),
        name="star",
    )(count, pix, off, held, col_a, col_b, frac)


def spread_kernel(first, count, start, idx_ref, low_ref, here_ref, inner_ref, *refs):
    if start:
        start_hbm, refs = refs[0], refs[1:]
    out_hbm = refs[0]
    accs = refs[1:1 + ACCS]
    sem = refs[1 + ACCS]
    total_rows = out_hbm.shape[0]
    piece = total_rows // SPLIT

    if start:
        begin = pltpu.make_async_copy(start_hbm, accs[0], sem.at[SPLIT])
        begin.start()

    def clear(i, carry):
        for acc in accs[1 if start else 0:]:
            acc[pl.ds(pl.multiple_of(i * PACK, PACK), PACK), :] = jnp.zeros((PACK, LANES), jnp.float32)
        return carry

    lax.fori_loop(0, total_rows // PACK, clear, 0)
    if start:
        begin.wait()
    lane = lax.broadcasted_iota(jnp.int32, (SUB, LANES), 1)
    sub = lax.broadcasted_iota(jnp.int32, (SUB, LANES), 0)
    pair = sub >> 1
    in_pair = [pair == j for j in range(4)]
    even = (sub & 1) == 0

    def body(o, carry):
        def row_of(ref):
            return jnp.broadcast_to(ref[pl.ds(o, 1), :], (SUB, LANES))

        low = row_of(low_ref)
        value = jnp.where(even, row_of(inner_ref), row_of(here_ref))
        for k in range(LANES // 4):
            at = pair + 4 * k
            here = jnp.take_along_axis(low, at, axis=1) == lane
            four = jnp.where(here, jnp.take_along_axis(value, at, axis=1), 0.0)
            for j in range(4):
                acc = accs[(4 * k + j) % ACCS]
                rows = pl.ds(idx_ref[o, 4 * k + j] - 2 * j, SUB)
                acc[rows, :] = acc[rows, :] + jnp.where(in_pair[j], four, 0.0)
        return carry

    lax.fori_loop(first, first + count, body, 0)

    copies = []
    for i in range(SPLIT):
        def gather(k, carry, i=i):
            rows = pl.ds(pl.multiple_of(i * piece + k * PACK, PACK), PACK)
            total = accs[0][rows, :]
            for acc in accs[1:]:
                total = total + acc[rows, :]
            accs[0][rows, :] = total
            return carry

        lax.fori_loop(0, piece // PACK, gather, 0)
        part = pl.ds(i * piece, piece)
        copy = pltpu.make_async_copy(accs[0].at[part, :], out_hbm.at[part, :], sem.at[i])
        copy.start()
        copies.append(copy)
    for copy in copies:
        copy.wait()


def spread_call(idx, low, here, inner, rows, first, count, start=None):
    shape = (rows, LANES)
    extra = () if start is None else (start,)
    return pl.pallas_call(
        lambda *refs: spread_kernel(first, count, start is not None, *refs),
        out_shape=jax.ShapeDtypeStruct(shape, jnp.float32),
        in_specs=[SMEM, VMEM, VMEM, VMEM] + [ANY] * len(extra),
        out_specs=ANY,
        scratch_shapes=[pltpu.VMEM(shape, jnp.float32)] * ACCS + [pltpu.SemaphoreType.DMA((SPLIT + 1,))],
        cost_estimate=cost(20, 5 << 20),
        name="spread",
    )(idx, low, here, inner, *extra)


def chunked(work, inputs, outputs):
    for i in range(CHUNKS):
        for copy in inputs(i):
            copy.start()

    def step(i, carry):
        for copy in inputs(i):
            copy.wait()
        work(i)
        for copy in outputs(i):
            copy.start()
        return carry

    lax.fori_loop(0, CHUNKS, step, 0)
    for i in range(CHUNKS):
        for copy in outputs(i):
            copy.wait()


def extinction_kernel(shells, devices, off_ref, tab_hbm, out_hbm, tab_ref, out_ref, in_sem, out_sem):
    tall = shells + 1
    groups = off_ref.shape[0]
    per = groups // CHUNKS

    def inputs(i):
        rows = pl.ds(LEAD + i * per * tall, per * tall)
        return [pltpu.make_async_copy(tab_hbm.at[rows, :], tab_ref.at[rows, :], in_sem.at[i])]

    def outputs(i):
        rows = pl.ds(i * per * SUB, per * SUB)
        return [pltpu.make_async_copy(out_ref.at[:, rows, :], out_hbm.at[:, rows, :], out_sem.at[i])]

    def work(i):
        for k in range(per):
            g = i * per + k
            off = off_ref[pl.ds((g % devices) * (groups // devices) + g // devices, 1), :]
            for b in range(shells // SUB):
                value = tab_ref[pl.ds(LEAD + g * tall + 1 + b * SUB, SUB), :] + off
                out_ref[b, pl.ds(pl.multiple_of(g * SUB, SUB), SUB), :] = value

    chunked(work, inputs, outputs)


def extinction_call(tab, off, shells, devices):
    shape = (shells // SUB, off.shape[0] * SUB, LANES)
    return pl.pallas_call(
        lambda *refs: extinction_kernel(shells, devices, *refs),
        in_specs=[VMEM, ANY],
        out_specs=ANY,
        out_shape=jax.ShapeDtypeStruct(shape, jnp.float32),
        scratch_shapes=[
            pltpu.VMEM(tab.shape, jnp.float32),
            pltpu.VMEM(shape, jnp.float32),
            pltpu.SemaphoreType.DMA((CHUNKS,)),
            pltpu.SemaphoreType.DMA((CHUNKS,)),
        ],
        cost_estimate=cost(4, 8 << 20),
        name="extinction",
    )(off, tab)


def sensitivity_kernel(shells, devices, off_ref, dens_hbm, drop_hbm, out_hbm, dens_ref, drop_ref, out_ref,
                       in_sem, out_sem):
    tall = shells + 1
    groups = off_ref.shape[0]
    share = groups // devices
    per = groups // CHUNKS

    def inputs(i):
        flat = pl.ds(i * per * shells, per * shells)
        rows = pl.ds(LEAD + i * per * tall, per * tall)
        return [
            pltpu.make_async_copy(dens_hbm.at[flat, :], dens_ref.at[flat, :], in_sem.at[0, i]),
            pltpu.make_async_copy(drop_hbm.at[rows, :], drop_ref.at[rows, :], in_sem.at[1, i]),
        ]

    def outputs(i):
        rows = pl.ds(i * per * SUB, per * SUB)
        return [pltpu.make_async_copy(out_ref.at[:, rows, :], out_hbm.at[:, rows, :], out_sem.at[i])]

    def work(i):
        for k in range(per // SUB):
            g = i * (per // SUB) + k
            first = g * SUB
            total = off_ref[pl.ds((first % devices) * share + first // devices, SUB, stride=share), :]
            for r in range(shells - 1, -1, -1):
                total = total + drop_ref[pl.ds(LEAD + g * SUB * tall + 1 + r, SUB, stride=tall), :]
                out_ref.at[r // SUB][pl.ds(g * SUB * SUB + r % SUB, SUB, stride=SUB), :] = (
                    dens_ref[pl.ds((g * shells + r) * SUB, SUB), :] * total)

    chunked(work, inputs, outputs)


def sensitivity_call(dens, drop, off, shells, devices):
    shape = (shells // SUB, off.shape[0] * SUB, LANES)
    return pl.pallas_call(
        lambda *refs: sensitivity_kernel(shells, devices, *refs),
        in_specs=[VMEM, ANY, ANY],
        out_specs=ANY,
        out_shape=jax.ShapeDtypeStruct(shape, jnp.float32),
        scratch_shapes=[
            pltpu.VMEM(dens.shape, jnp.float32),
            pltpu.VMEM(drop.shape, jnp.float32),
            pltpu.VMEM(shape, jnp.float32),
            pltpu.SemaphoreType.DMA((2, CHUNKS)),
            pltpu.SemaphoreType.DMA((CHUNKS,)),
        ],
        cost_estimate=cost(5, 12 << 20),
        name="sensitivity",
    )(off, dens, drop)


def to_tiles(x):
    shells, pixels = x.shape
    groups = pixels // LANES
    x = x.reshape(shells // SUB, SUB, groups, LANES).transpose(0, 2, 1, 3)
    return x.reshape(shells // SUB, groups * SUB, LANES)


def from_tiles(x):
    bands, rows, lanes = x.shape
    groups = rows // SUB
    x = x.reshape(bands, groups, SUB, lanes).transpose(0, 2, 1, 3)
    return x.reshape(bands * SUB, groups * lanes)


def edge_rows(x, rows):
    count, pixels = rows.stop - rows.start, x.shape[1]
    part = x[rows].reshape(count, pixels // LANES, LANES).transpose(1, 0, 2)
    return part


def body(excitation, star_shell, star_pixel, star_fraction, star_count, observed, inverse_error):
    shells, pixels = excitation.shape
    blocks = lax.axis_size("shell")
    devices = blocks * lax.axis_size("sky")
    me = lax.axis_index("shell")
    thickness = depth_span / (shells * blocks)
    groups = pixels // LANES
    tall = shells + 1
    owners = star_shell.shape[1]

    up = [(i, i + 1) for i in range(blocks - 1)]
    down = [(i + 1, i) for i in range(blocks - 1)]
    from_below = lax.ppermute(edge_rows(excitation, slice(shells - PASSES, shells)), "shell", up)
    from_above = lax.ppermute(edge_rows(excitation, slice(0, PASSES)), "shell", down)

    pixel, fraction = star_pixel[0], star_fraction[0]
    low = pixel & (LANES - 1)
    idx = (pixel >> 7) * tall + star_shell[0] + LEAD
    edge = jnp.stack(((me == 0).astype(jnp.float32), (me == blocks - 1).astype(jnp.float32)))
    dens, tab, parts = density_call(
        to_tiles(excitation),
        from_below.reshape(groups * PASSES, LANES),
        from_above.reshape(groups * PASSES, LANES),
        edge, observed[:, 0], inverse_error[:, 0], shells, groups, devices, thickness)

    held = exchange(parts, devices)
    offset = exchange(scan_call(held, devices, False, False)[0], devices)
    half = owners // 2
    col_a = lookup_call(idx, tab, low, fraction, 0, half)
    col_b = lookup_call(idx, tab, low, fraction, half, owners - half)

    parts, here, inner = star_call(star_count, pixel, offset, held, col_a, col_b, fraction, devices)
    sums, residual = scan_call(exchange(parts, devices), devices, True, True)
    tail_offset = exchange(sums, devices)

    rows = table_rows(groups, tall)
    drop = spread_call(idx, low, here, inner, rows, 0, half)
    drop = spread_call(idx, low, here, inner, rows, half, owners - half, drop)
    extinction = extinction_call(tab, offset, shells, devices)
    sensitivity = sensitivity_call(dens, drop, tail_offset, shells, devices)
    return from_tiles(extinction), from_tiles(sensitivity), residual[:, None, :]


def solution(mesh):
    placed = (
        P("shell", "sky"),
        P(BOTH, None, None),
        P(BOTH, None, None),
        P(BOTH, None, None),
        P(BOTH, None),
        P(None, BOTH, None),
        P(None, BOTH, None),
    )
    return jax.shard_map(
        body,
        mesh=mesh,
        in_specs=placed,
        out_specs=(P("shell", "sky"), P("shell", "sky"), P(None, BOTH, None)),
        check_vma=False,
    )
```

```python
import jax
import jax.numpy as jnp
from jax import lax
from jax.experimental import pallas as pl
from jax.experimental.pallas import tpu as pltpu
from jax.sharding import PartitionSpec as P

PASSES = 4
LANES = 128
SUB = 8
LEAD = 8
ACCS = 5
TEAM = 4
PAIR = 2
STEP = 32
CHUNKS = 8
SPLIT = 7
PACK = 64
FIELDS = 4
BOTH = ("shell", "sky")


depth_span = 2.0

VMEM = pl.BlockSpec(memory_space=pltpu.VMEM)
SMEM = pl.BlockSpec(memory_space=pltpu.SMEM)
ANY = pl.BlockSpec(memory_space=pl.ANY)


def cost(micros, nbytes):
    return pl.CostEstimate(flops=int(micros * 2e8), bytes_accessed=int(nbytes), transcendentals=0)


def taps():
    power = [1.0]
    total = [0.0] * (2 * PASSES + 1)
    for k in range(PASSES + 1):
        for i, v in enumerate(power):
            total[PASSES - k + i] += v
        wider = [0.0] * (len(power) + 2)
        for i, v in enumerate(power):
            wider[i] += 0.3 * v
            wider[i + 1] += 0.35 * v
            wider[i + 2] += 0.3 * v
        power = wider
    return total[PASSES:]


def table_rows(groups, tall):
    unit = SPLIT * PACK
    return -(-(LEAD + groups * tall + SUB) // unit) * unit


def density_kernel(shells, groups, devices, thickness, edge_ref, obs_ref, inv_ref, exc_hbm, up_hbm, down_hbm,
                   dens_hbm, tab_hbm, pay_ref, exc_ref, up_ref, down_ref, dens_ref, tab_ref, in_sem, out_sem):
    tall = shells + 1
    per = groups // CHUNKS
    weight = taps()
    low_edge = edge_ref[0]
    high_edge = edge_ref[1]

    def inputs(i):
        wide = pl.ds(i * per * SUB, per * SUB)
        thin = pl.ds(i * per * PASSES, per * PASSES)
        return [
            pltpu.make_async_copy(exc_hbm.at[:, wide, :], exc_ref.at[:, wide, :], in_sem.at[0, i]),
            pltpu.make_async_copy(up_hbm.at[thin, :], up_ref.at[thin, :], in_sem.at[1, i]),
            pltpu.make_async_copy(down_hbm.at[thin, :], down_ref.at[thin, :], in_sem.at[2, i]),
        ]

    def outputs(i):
        flat = pl.ds(i * per * shells, per * shells)
        tall_rows = pl.ds(LEAD + i * per * tall, per * tall)
        return [
            pltpu.make_async_copy(dens_ref.at[flat, :], dens_hbm.at[flat, :], out_sem.at[0, i]),
            pltpu.make_async_copy(tab_ref.at[tall_rows, :], tab_hbm.at[tall_rows, :], out_sem.at[1, i]),
        ]

    for i in range(CHUNKS):
        for copy in inputs(i):
            copy.start()
    pay_ref[pl.ds(0, devices, stride=FIELDS), :] = obs_ref[...]
    pay_ref[pl.ds(1, devices, stride=FIELDS), :] = inv_ref[...]

    def group(g):
        exc = {}
        for r in range(shells):
            exc[r] = exc_ref.at[r // SUB][pl.ds(g * SUB * SUB + r % SUB, SUB, stride=SUB), :]
        for k in range(PASSES):
            low = up_ref[pl.ds(g * SUB * PASSES + PASSES - 1 - k, SUB, stride=PASSES), :]
            high = down_ref[pl.ds(g * SUB * PASSES + k, SUB, stride=PASSES), :]
            if k:
                low = low - low_edge * exc[k - 1]
                high = high - high_edge * exc[shells - k]
            exc[-1 - k] = low
            exc[shells + k] = high
        tab_ref[pl.ds(LEAD + g * SUB * tall, SUB, stride=tall), :] = jnp.zeros((SUB, LANES), jnp.float32)
        total = None
        for r in range(shells):
            value = weight[0] * exc[r]
            for k in range(1, PASSES + 1):
                value = value + weight[k] * (exc[r - k] + exc[r + k])
            dens = jnp.exp(value)
            dens_ref[pl.ds((g * shells + r) * SUB, SUB), :] = dens
            step = dens * thickness
            total = step if total is None else total + step
            tab_ref[pl.ds(LEAD + g * SUB * tall + 1 + r, SUB, stride=tall), :] = total
        first = g * SUB
        pay_ref[pl.ds((first % devices) * FIELDS + 2 + first // devices, SUB, stride=FIELDS), :] = total

    def chunk(i, carry):
        for copy in inputs(i):
            copy.wait()
        for k in range(per // SUB):
            group(i * (per // SUB) + k)
        for copy in outputs(i):
            copy.start()
        return carry

    lax.fori_loop(0, CHUNKS, chunk, 0)
    for i in range(CHUNKS):
        for copy in outputs(i):
            copy.wait()


def density_call(exc, up, down, edge, obs, inv, shells, groups, devices, thickness):
    tall = shells + 1
    rows = table_rows(groups, tall)
    return pl.pallas_call(
        lambda *refs: density_kernel(shells, groups, devices, thickness, *refs),
        in_specs=[SMEM, VMEM, VMEM, ANY, ANY, ANY],
        out_specs=[ANY, ANY, VMEM],
        out_shape=[
            jax.ShapeDtypeStruct((groups * shells, LANES), jnp.float32),
            jax.ShapeDtypeStruct((rows, LANES), jnp.float32),
            jax.ShapeDtypeStruct((devices * FIELDS, LANES), jnp.float32),
        ],
        scratch_shapes=[
            pltpu.VMEM(exc.shape, jnp.float32),
            pltpu.VMEM(up.shape, jnp.float32),
            pltpu.VMEM(down.shape, jnp.float32),
            pltpu.VMEM((groups * shells, LANES), jnp.float32),
            pltpu.VMEM((rows, LANES), jnp.float32),
            pltpu.SemaphoreType.DMA((3, CHUNKS)),
            pltpu.SemaphoreType.DMA((2, CHUNKS)),
        ],
        cost_estimate=cost(8, 12 << 20),
        name="density",
    )(edge, obs, inv, exc, up, down)


def team_sizes(team, first, count_ref, work):
    steps = lax.div(count_ref[1, first] + (STEP - 1), STEP)
    for size in range(1, LANES // STEP + 1):
        @pl.when(steps == size)
        def _(size=size):
            work([count_ref[0, first + t] for t in range(team)], size * STEP)


def lookup_kernel(part, parts, chained, count_ref, idx_ref, tab_ref, low_ref, frac_ref, *refs):
    out_ref = refs[-1]
    out_ref[...] = refs[0][...] if chained else jnp.zeros_like(out_ref)
    lane = lax.broadcasted_iota(jnp.int32, (SUB, LANES), 1)
    sub = lax.broadcasted_iota(jnp.int32, (SUB, LANES), 0)
    pair = [(sub >> 1) == j for j in range(4)]
    quad = lane >> 2
    is_inner = sub == (lane & 3) * 2
    is_outer = sub == (lane & 3) * 2 + 1

    def work(owners, slots):
        low = [jnp.broadcast_to(low_ref[pl.ds(o, 1), :], (SUB, LANES)) for o in owners]
        at = [idx_ref.at[o] for o in owners]
        got = [jnp.zeros((SUB, LANES), jnp.float32) for _ in owners]
        for k in range(slots // 4):
            rows = [None] * len(owners)
            for j in range(4):
                for t in range(len(owners)):
                    value = tab_ref[pl.ds(at[t][4 * k + j] - 2 * j, SUB), :]
                    rows[t] = value if j == 0 else jnp.where(pair[j], value, rows[t])
            for t in range(len(owners)):
                got[t] = jnp.where(quad == k, jnp.take_along_axis(rows[t], low[t], axis=1), got[t])
        for t, o in enumerate(owners):
            inner = jnp.sum(jnp.where(is_inner, got[t], 0.0), axis=0, keepdims=True)
            outer = jnp.sum(jnp.where(is_outer, got[t], 0.0), axis=0, keepdims=True)
            out_ref[pl.ds(o, 1), :] = inner + frac_ref[pl.ds(o, 1), :] * (outer - inner)

    def body(i, carry):
        team_sizes(TEAM, (i * parts + part) * TEAM, count_ref, work)
        return carry

    lax.fori_loop(0, out_ref.shape[0] // (TEAM * parts), body, 0)


def lookup_call(counts, idx, tab, low, frac, part, parts, column=None):
    extra = () if column is None else (column,)
    return pl.pallas_call(
        lambda *refs: lookup_kernel(part, parts, column is not None, *refs),
        out_shape=jax.ShapeDtypeStruct(low.shape, jnp.float32),
        in_specs=[SMEM, SMEM] + [VMEM] * (3 + len(extra)),
        out_specs=VMEM,
        cost_estimate=cost(12, 5 << 20),
        name="lookup",
    )(counts, idx, tab, low, frac, *extra)


def scan_kernel(reverse, in_ref, out_ref, *field_ref):
    blocks = in_ref.shape[0] // SUB
    total = jnp.zeros((SUB, LANES), jnp.float32)
    for b in range(blocks - 1, -1, -1) if reverse else range(blocks):
        out_ref[4 * b:4 * b + 2, :] = total[2:4]
        out_ref[4 * b + 2:4 * b + 4, :] = total[6:8]
        total = total + in_ref[SUB * b:SUB * (b + 1), :]
    if field_ref:
        field_ref[0][...] = in_ref[pl.ds(0, field_ref[0].shape[0], stride=FIELDS), :]


def scan_call(parts, devices, reverse, field):
    shapes = [jax.ShapeDtypeStruct((devices * (FIELDS - 2), LANES), jnp.float32)]
    if field:
        shapes.append(jax.ShapeDtypeStruct((devices, LANES), jnp.float32))
    return pl.pallas_call(
        lambda *refs: scan_kernel(reverse, *refs),
        out_shape=shapes,
        cost_estimate=cost(1, 1 << 18),
        name="scan",
    )(parts)


def exchange(rows, devices):
    parts = rows.reshape(devices, rows.shape[0] // devices, LANES)
    parts = lax.all_to_all(parts, BOTH, split_axis=0, concat_axis=0, tiled=True)
    return parts.reshape(rows.shape)


def halves(x):
    high = x.astype(jnp.bfloat16)
    return high, (x - high.astype(jnp.float32)).astype(jnp.bfloat16)


def star_kernel(devices, count_ref, pix_ref, off_ref, held_ref, col_ref, frac_ref,
                pay_ref, here_ref, inner_ref, acc_ref, tail_ref):
    groups = off_ref.shape[0]
    rows = SUB
    offt = jnp.transpose(off_ref[...])
    offt = jnp.concatenate(halves(offt), axis=0)
    group_id = lax.broadcasted_iota(jnp.int32, (groups, LANES), 0).astype(jnp.bfloat16)
    lane_id = lax.broadcasted_iota(jnp.int32, (LANES, LANES), 0)
    slot = lax.broadcasted_iota(jnp.int32, (rows, LANES), 1)
    sub = lax.broadcasted_iota(jnp.int32, (rows, LANES), 0)
    one = jnp.ones((groups, LANES), jnp.bfloat16)
    zero = jnp.zeros((groups, LANES), jnp.bfloat16)
    acc_ref[...] = jnp.zeros_like(acc_ref)
    pay_ref[pl.ds(1, devices, stride=FIELDS), :] = jnp.zeros((devices, LANES), jnp.float32)

    def body(b):
        at = pl.ds(pl.multiple_of(b * rows, rows), rows)
        pix = pix_ref[at, :]
        high = lax.shift_right_logical(pix, 7)
        high = (lax.rem(high, devices)) * (groups // devices) + lax.div(high, devices)
        high = high.astype(jnp.float32).astype(jnp.bfloat16)
        low = pix & 127
        pick = jnp.concatenate([jnp.where(group_id == high[j:j + 1, :], one, zero) for j in range(rows)], axis=1)
        found = jnp.dot(offt, pick, preferred_element_type=jnp.float32)
        lanes = [lane_id == low[j:j + 1, :] for j in range(rows)]
        off_at = []
        for j in range(rows):
            part = found[:, j * LANES:(j + 1) * LANES]
            part = jnp.where(lanes[j], part[:LANES] + part[LANES:], 0.0)
            off_at.append(jnp.sum(part, axis=0, keepdims=True))
        column = col_ref[at, :] + jnp.concatenate(off_at, axis=0)
        obs = held_ref[pl.ds(b * rows * FIELDS, rows, stride=FIELDS), :]
        inv = held_ref[pl.ds(b * rows * FIELDS + 1, rows, stride=FIELDS), :]
        live = jnp.zeros((rows, LANES), jnp.int32)
        for j in range(rows):
            live = jnp.where(sub == j, count_ref[0, b * rows + j], live)
        transmit = jnp.exp(-jnp.where(slot < live, column, 0.0))
        residual = jnp.where(slot < live, (obs - (1.0 - transmit)) * inv, 0.0)
        pull = -residual * inv * transmit
        inner = (1.0 - frac_ref[at, :]) * pull
        pay_ref[pl.ds(b * rows * FIELDS, rows, stride=FIELDS), :] = residual
        here_ref[at, :] = pull - inner
        inner_ref[at, :] = inner
        spread = []
        for j in range(rows):
            spread.append(jnp.concatenate(halves(jnp.where(lanes[j], pull[j:j + 1, :], 0.0)), axis=0))
        spread = jnp.concatenate(spread, axis=1)
        acc_ref[...] += lax.dot_general(
            pick, spread, (((1,), (1,)), ((), ())), preferred_element_type=jnp.float32)

    @pl.loop(0, pix_ref.shape[0] // (2 * rows))
    def _(b):
        body(2 * b)
        body(2 * b + 1)

    tail_ref[...] = acc_ref[:, :LANES] + acc_ref[:, LANES:]
    for e in range(groups // devices):
        pay_ref[pl.ds(2 + e, devices, stride=FIELDS), :] = tail_ref[pl.ds(e, devices, stride=groups // devices), :]


def star_call(count, pix, off, held, column, frac, devices):
    slots = jax.ShapeDtypeStruct(pix.shape, jnp.float32)
    return pl.pallas_call(
        lambda *refs: star_kernel(devices, *refs),
        out_shape=[jax.ShapeDtypeStruct(held.shape, jnp.float32), slots, slots],
        in_specs=[SMEM] + [VMEM] * 5,
        out_specs=[VMEM] * 3,
        scratch_shapes=[pltpu.VMEM((off.shape[0], 2 * LANES), jnp.float32), pltpu.VMEM(off.shape, jnp.float32)],
        cost_estimate=cost(8, 1 << 20),
        name="star",
    )(count, pix, off, held, column, frac)


def spread_kernel(count_ref, idx_ref, low_ref, here_ref, inner_ref, out_hbm, *refs):
    accs = refs[:ACCS]
    sem = refs[ACCS]
    total_rows = out_hbm.shape[0]
    piece = total_rows // SPLIT

    def clear(i, carry):
        for acc in accs:
            acc[pl.ds(pl.multiple_of(i * PACK, PACK), PACK), :] = jnp.zeros((PACK, LANES), jnp.float32)
        return carry

    lax.fori_loop(0, total_rows // PACK, clear, 0)
    lane = lax.broadcasted_iota(jnp.int32, (SUB, LANES), 1)
    sub = lax.broadcasted_iota(jnp.int32, (SUB, LANES), 0)
    pair = sub >> 1
    in_pair = [pair == j for j in range(4)]
    even = (sub & 1) == 0

    def work(owners, slots):
        def row_of(ref, o):
            return jnp.broadcast_to(ref[pl.ds(o, 1), :], (SUB, LANES))

        low = [row_of(low_ref, o) for o in owners]
        value = [jnp.where(even, row_of(inner_ref, o), row_of(here_ref, o)) for o in owners]
        at = [idx_ref.at[o] for o in owners]
        turn = 0
        for k in range(slots // 4):
            pick = pair + 4 * k
            four = []
            for t in range(len(owners)):
                here = jnp.take_along_axis(low[t], pick, axis=1) == lane
                four.append(jnp.where(here, jnp.take_along_axis(value[t], pick, axis=1), 0.0))
            for j in range(4):
                for t in range(len(owners)):
                    acc = accs[turn % ACCS]
                    turn += 1
                    rows = pl.ds(at[t][4 * k + j] - 2 * j, SUB)
                    acc[rows, :] = acc[rows, :] + jnp.where(in_pair[j], four[t], 0.0)

    def body(i, carry):
        team_sizes(PAIR, i * PAIR, count_ref, work)
        return carry

    lax.fori_loop(0, idx_ref.shape[0] // PAIR, body, 0)

    copies = []
    for i in range(SPLIT):
        def gather(k, carry, i=i):
            rows = pl.ds(pl.multiple_of(i * piece + k * PACK, PACK), PACK)
            total = accs[0][rows, :]
            for acc in accs[1:]:
                total = total + acc[rows, :]
            accs[0][rows, :] = total
            return carry

        lax.fori_loop(0, piece // PACK, gather, 0)
        part = pl.ds(i * piece, piece)
        copy = pltpu.make_async_copy(accs[0].at[part, :], out_hbm.at[part, :], sem.at[i])
        copy.start()
        copies.append(copy)
    for copy in copies:
        copy.wait()


def spread_call(counts, idx, low, here, inner, rows):
    shape = (rows, LANES)
    return pl.pallas_call(
        spread_kernel,
        out_shape=jax.ShapeDtypeStruct(shape, jnp.float32),
        in_specs=[SMEM, SMEM, VMEM, VMEM, VMEM],
        out_specs=ANY,
        scratch_shapes=[pltpu.VMEM(shape, jnp.float32)] * ACCS + [pltpu.SemaphoreType.DMA((SPLIT,))],
        cost_estimate=cost(30, 5 << 20),
        name="spread",
    )(counts, idx, low, here, inner)


def chunked(work, inputs, outputs):
    for i in range(CHUNKS):
        for copy in inputs(i):
            copy.start()

    def step(i, carry):
        for copy in inputs(i):
            copy.wait()
        work(i)
        for copy in outputs(i):
            copy.start()
        return carry

    lax.fori_loop(0, CHUNKS, step, 0)
    for i in range(CHUNKS):
        for copy in outputs(i):
            copy.wait()


def extinction_kernel(shells, devices, off_ref, tab_hbm, out_hbm, tab_ref, out_ref, in_sem, out_sem):
    tall = shells + 1
    groups = off_ref.shape[0]
    per = groups // CHUNKS

    def inputs(i):
        rows = pl.ds(LEAD + i * per * tall, per * tall)
        return [pltpu.make_async_copy(tab_hbm.at[rows, :], tab_ref.at[rows, :], in_sem.at[i])]

    def outputs(i):
        rows = pl.ds(i * per * SUB, per * SUB)
        return [pltpu.make_async_copy(out_ref.at[:, rows, :], out_hbm.at[:, rows, :], out_sem.at[i])]

    def work(i):
        for k in range(per):
            g = i * per + k
            off = off_ref[pl.ds((g % devices) * (groups // devices) + g // devices, 1), :]
            for b in range(shells // SUB):
                value = tab_ref[pl.ds(LEAD + g * tall + 1 + b * SUB, SUB), :] + off
                out_ref[b, pl.ds(pl.multiple_of(g * SUB, SUB), SUB), :] = value

    chunked(work, inputs, outputs)


def extinction_call(tab, off, shells, devices):
    shape = (shells // SUB, off.shape[0] * SUB, LANES)
    return pl.pallas_call(
        lambda *refs: extinction_kernel(shells, devices, *refs),
        in_specs=[VMEM, ANY],
        out_specs=ANY,
        out_shape=jax.ShapeDtypeStruct(shape, jnp.float32),
        scratch_shapes=[
            pltpu.VMEM(tab.shape, jnp.float32),
            pltpu.VMEM(shape, jnp.float32),
            pltpu.SemaphoreType.DMA((CHUNKS,)),
            pltpu.SemaphoreType.DMA((CHUNKS,)),
        ],
        cost_estimate=cost(4, 8 << 20),
        name="extinction",
    )(off, tab)


def sensitivity_kernel(shells, devices, off_ref, dens_hbm, drop_hbm, out_hbm, dens_ref, drop_ref, out_ref,
                       in_sem, out_sem):
    tall = shells + 1
    groups = off_ref.shape[0]
    share = groups // devices
    per = groups // CHUNKS

    def inputs(i):
        flat = pl.ds(i * per * shells, per * shells)
        rows = pl.ds(LEAD + i * per * tall, per * tall)
        return [
            pltpu.make_async_copy(dens_hbm.at[flat, :], dens_ref.at[flat, :], in_sem.at[0, i]),
            pltpu.make_async_copy(drop_hbm.at[rows, :], drop_ref.at[rows, :], in_sem.at[1, i]),
        ]

    def outputs(i):
        rows = pl.ds(i * per * SUB, per * SUB)
        return [pltpu.make_async_copy(out_ref.at[:, rows, :], out_hbm.at[:, rows, :], out_sem.at[i])]

    def work(i):
        for k in range(per // SUB):
            g = i * (per // SUB) + k
            first = g * SUB
            total = off_ref[pl.ds((first % devices) * share + first // devices, SUB, stride=share), :]
            for r in range(shells - 1, -1, -1):
                total = total + drop_ref[pl.ds(LEAD + g * SUB * tall + 1 + r, SUB, stride=tall), :]
                out_ref.at[r // SUB][pl.ds(g * SUB * SUB + r % SUB, SUB, stride=SUB), :] = (
                    dens_ref[pl.ds((g * shells + r) * SUB, SUB), :] * total)

    chunked(work, inputs, outputs)


def sensitivity_call(dens, drop, off, shells, devices):
    shape = (shells // SUB, off.shape[0] * SUB, LANES)
    return pl.pallas_call(
        lambda *refs: sensitivity_kernel(shells, devices, *refs),
        in_specs=[VMEM, ANY, ANY],
        out_specs=ANY,
        out_shape=jax.ShapeDtypeStruct(shape, jnp.float32),
        scratch_shapes=[
            pltpu.VMEM(dens.shape, jnp.float32),
            pltpu.VMEM(drop.shape, jnp.float32),
            pltpu.VMEM(shape, jnp.float32),
            pltpu.SemaphoreType.DMA((2, CHUNKS)),
            pltpu.SemaphoreType.DMA((CHUNKS,)),
        ],
        cost_estimate=cost(5, 12 << 20),
        name="sensitivity",
    )(off, dens, drop)


def to_tiles(x):
    shells, pixels = x.shape
    groups = pixels // LANES
    x = x.reshape(shells // SUB, SUB, groups, LANES).transpose(0, 2, 1, 3)
    return x.reshape(shells // SUB, groups * SUB, LANES)


def from_tiles(x):
    bands, rows, lanes = x.shape
    groups = rows // SUB
    x = x.reshape(bands, groups, SUB, lanes).transpose(0, 2, 1, 3)
    return x.reshape(bands * SUB, groups * lanes)


def edge_rows(x, rows):
    count, pixels = rows.stop - rows.start, x.shape[1]
    part = x[rows].reshape(count, pixels // LANES, LANES).transpose(1, 0, 2)
    return part


def sorted_owners(count):
    n = count.shape[0]
    a = lax.broadcasted_iota(jnp.int32, (n, n), 0)
    b = lax.broadcasted_iota(jnp.int32, (n, n), 1)
    ahead = (count[None, :] > count[:, None]) | ((count[None, :] == count[:, None]) & (b < a))
    place = jnp.sum(ahead.astype(jnp.int32), axis=1)
    mine = place[None, :] == a
    return jnp.stack((jnp.sum(jnp.where(mine, b, 0), axis=1), jnp.sum(jnp.where(mine, count[None, :], 0), axis=1)))


def body(excitation, star_shell, star_pixel, star_fraction, star_count, observed, inverse_error):
    shells, pixels = excitation.shape
    blocks = lax.axis_size("shell")
    devices = blocks * lax.axis_size("sky")
    me = lax.axis_index("shell")
    thickness = depth_span / (shells * blocks)
    groups = pixels // LANES
    tall = shells + 1

    up = [(i, i + 1) for i in range(blocks - 1)]
    down = [(i + 1, i) for i in range(blocks - 1)]
    from_below = lax.ppermute(edge_rows(excitation, slice(shells - PASSES, shells)), "shell", up)
    from_above = lax.ppermute(edge_rows(excitation, slice(0, PASSES)), "shell", down)

    pixel, fraction = star_pixel[0], star_fraction[0]
    low = pixel & (LANES - 1)
    idx = (pixel >> 7) * tall + star_shell[0] + LEAD
    counts = sorted_owners(star_count[0])
    edge = jnp.stack(((me == 0).astype(jnp.float32), (me == blocks - 1).astype(jnp.float32)))
    dens, tab, parts = density_call(
        to_tiles(excitation),
        from_below.reshape(groups * PASSES, LANES),
        from_above.reshape(groups * PASSES, LANES),
        edge, observed[:, 0], inverse_error[:, 0], shells, groups, devices, thickness)

    held = exchange(parts, devices)
    offset = exchange(scan_call(held, devices, False, False)[0], devices)
    column = lookup_call(counts, idx, tab, low, fraction, 0, 2)
    column = lookup_call(counts, idx, tab, low, fraction, 1, 2, column)

    parts, here, inner = star_call(star_count, pixel, offset, held, column, fraction, devices)
    extinction = extinction_call(tab, offset, shells, devices)
    parts, extinction = lax.optimization_barrier((exchange(parts, devices), extinction))
    sums, residual = scan_call(parts, devices, True, True)
    tail_offset = exchange(sums, devices)

    rows = table_rows(groups, tall)
    drop = spread_call(counts, idx, low, here, inner, rows)
    sensitivity = sensitivity_call(dens, drop, tail_offset, shells, devices)
    return from_tiles(extinction), from_tiles(sensitivity), residual[:, None, :]


def solution(mesh):
    placed = (
        P("shell", "sky"),
        P(BOTH, None, None),
        P(BOTH, None, None),
        P(BOTH, None, None),
        P(BOTH, None),
        P(None, BOTH, None),
        P(None, BOTH, None),
    )
    return jax.shard_map(
        body,
        mesh=mesh,
        in_specs=placed,
        out_specs=(P("shell", "sky"), P("shell", "sky"), P(None, BOTH, None)),
        check_vma=False,
    )
```

```python
import math
import jax
import jax.numpy as jnp
from jax import lax
from jax.experimental import pallas as pl
from jax.experimental.pallas import tpu as pltpu
from jax.sharding import PartitionSpec as P

PASSES = 4
LANES = 128
SUB = 8
LEAD = 8
ACCS = 6
TEAM = 4
PAIR = 2
STEP = 32
CHUNKS = 8
SPLIT = 7
PACK = 64
FIELDS = 4
LOG2E = math.log2(math.e)
BOTH = ("shell", "sky")


depth_span = 2.0

VMEM = pl.BlockSpec(memory_space=pltpu.VMEM)
SMEM = pl.BlockSpec(memory_space=pltpu.SMEM)
ANY = pl.BlockSpec(memory_space=pl.ANY)


def cost(micros, nbytes):
    return pl.CostEstimate(flops=int(micros * 2e8), bytes_accessed=int(nbytes), transcendentals=0)


def taps():
    power = [1.0]
    total = [0.0] * (2 * PASSES + 1)
    for k in range(PASSES + 1):
        for i, v in enumerate(power):
            total[PASSES - k + i] += v
        wider = [0.0] * (len(power) + 2)
        for i, v in enumerate(power):
            wider[i] += 0.3 * v
            wider[i + 1] += 0.35 * v
            wider[i + 2] += 0.3 * v
        power = wider
    return total[PASSES:]


def table_rows(groups, tall):
    unit = SPLIT * PACK
    return -(-(LEAD + groups * tall + SUB) // unit) * unit


def density_kernel(shells, groups, devices, thickness, edge_ref, obs_ref, inv_ref, exc_hbm, up_hbm, down_hbm,
                   dens_hbm, tab_hbm, pay_ref, exc_ref, up_ref, down_ref, dens_ref, tab_ref, in_sem, out_sem):
    tall = shells + 1
    per = groups // CHUNKS
    weight = [v * LOG2E for v in taps()]
    low_edge = edge_ref[0]
    high_edge = edge_ref[1]

    def inputs(i):
        wide = pl.ds(i * per * SUB, per * SUB)
        thin = pl.ds(i * per * PASSES, per * PASSES)
        return [
            pltpu.make_async_copy(exc_hbm.at[:, wide, :], exc_ref.at[:, wide, :], in_sem.at[0, i]),
            pltpu.make_async_copy(up_hbm.at[thin, :], up_ref.at[thin, :], in_sem.at[1, i]),
            pltpu.make_async_copy(down_hbm.at[thin, :], down_ref.at[thin, :], in_sem.at[2, i]),
        ]

    def outputs(i):
        flat = pl.ds(i * per * shells, per * shells)
        tall_rows = pl.ds(LEAD + i * per * tall, per * tall)
        return [
            pltpu.make_async_copy(dens_ref.at[flat, :], dens_hbm.at[flat, :], out_sem.at[0, i]),
            pltpu.make_async_copy(tab_ref.at[tall_rows, :], tab_hbm.at[tall_rows, :], out_sem.at[1, i]),
        ]

    for i in range(CHUNKS):
        for copy in inputs(i):
            copy.start()
    pay_ref[pl.ds(0, devices, stride=FIELDS), :] = obs_ref[...]
    pay_ref[pl.ds(1, devices, stride=FIELDS), :] = inv_ref[...]

    def group(g):
        exc = {}
        for r in range(shells):
            exc[r] = exc_ref.at[r // SUB][pl.ds(g * SUB * SUB + r % SUB, SUB, stride=SUB), :]
        for k in range(PASSES):
            low = up_ref[pl.ds(g * SUB * PASSES + PASSES - 1 - k, SUB, stride=PASSES), :]
            high = down_ref[pl.ds(g * SUB * PASSES + k, SUB, stride=PASSES), :]
            if k:
                low = low - low_edge * exc[k - 1]
                high = high - high_edge * exc[shells - k]
            exc[-1 - k] = low
            exc[shells + k] = high
        tab_ref[pl.ds(LEAD + g * SUB * tall, SUB, stride=tall), :] = jnp.zeros((SUB, LANES), jnp.float32)
        total = None
        for r in range(shells):
            value = weight[0] * exc[r]
            for k in range(1, PASSES + 1):
                value = value + weight[k] * (exc[r - k] + exc[r + k])
            dens = jnp.exp2(value)
            dens_ref[pl.ds((g * shells + r) * SUB, SUB), :] = dens
            step = dens * thickness
            total = step if total is None else total + step
            tab_ref[pl.ds(LEAD + g * SUB * tall + 1 + r, SUB, stride=tall), :] = total
        first = g * SUB
        pay_ref[pl.ds((first % devices) * FIELDS + 2 + first // devices, SUB, stride=FIELDS), :] = total

    def chunk(i, carry):
        for copy in inputs(i):
            copy.wait()
        for k in range(per // SUB):
            group(i * (per // SUB) + k)
        for copy in outputs(i):
            copy.start()
        return carry

    lax.fori_loop(0, CHUNKS, chunk, 0)
    for i in range(CHUNKS):
        for copy in outputs(i):
            copy.wait()


def density_call(exc, up, down, edge, obs, inv, shells, groups, devices, thickness):
    tall = shells + 1
    rows = table_rows(groups, tall)
    return pl.pallas_call(
        lambda *refs: density_kernel(shells, groups, devices, thickness, *refs),
        in_specs=[SMEM, VMEM, VMEM, ANY, ANY, ANY],
        out_specs=[ANY, ANY, VMEM],
        out_shape=[
            jax.ShapeDtypeStruct((groups * shells, LANES), jnp.float32),
            jax.ShapeDtypeStruct((rows, LANES), jnp.float32),
            jax.ShapeDtypeStruct((devices * FIELDS, LANES), jnp.float32),
        ],
        scratch_shapes=[
            pltpu.VMEM(exc.shape, jnp.float32),
            pltpu.VMEM(up.shape, jnp.float32),
            pltpu.VMEM(down.shape, jnp.float32),
            pltpu.VMEM((groups * shells, LANES), jnp.float32),
            pltpu.VMEM((rows, LANES), jnp.float32),
            pltpu.SemaphoreType.DMA((3, CHUNKS)),
            pltpu.SemaphoreType.DMA((2, CHUNKS)),
        ],
        cost_estimate=cost(8, 12 << 20),
        name="density",
    )(edge, obs, inv, exc, up, down)


def team_sizes(team, first, order_ref, count_ref, work):
    steps = lax.div(count_ref[first] + (STEP - 1), STEP)
    for size in range(1, LANES // STEP + 1):
        @pl.when(steps == size)
        def _(size=size):
            work([order_ref[first + t] for t in range(team)], size * STEP)


def fetch(sources, targets, sem):
    copies = [pltpu.make_async_copy(x, y, sem.at[i]) for i, (x, y) in enumerate(zip(sources, targets))]
    for copy in copies:
        copy.start()
    return copies


def lookup_kernel(part, parts, chained, order_ref, count_ref, *refs):
    n = 5 if chained else 4
    out_ref = refs[n]
    sources, targets, sem = refs[:n], refs[n + 1:-1], refs[-1]
    idx_ref, tab_ref, low_ref, frac_ref = targets
    if not chained:
        out_ref[...] = jnp.zeros_like(out_ref)
    for copy in fetch(sources, targets + ((out_ref,) if chained else ()), sem):
        copy.wait()
    lane = lax.broadcasted_iota(jnp.int32, (SUB, LANES), 1)
    sub = lax.broadcasted_iota(jnp.int32, (SUB, LANES), 0)
    pair = [(sub >> 1) == j for j in range(4)]
    quad = lane >> 2
    is_inner = sub == (lane & 3) * 2
    is_outer = sub == (lane & 3) * 2 + 1

    def work(owners, slots):
        low = [jnp.broadcast_to(low_ref[pl.ds(o, 1), :], (SUB, LANES)) for o in owners]
        at = [idx_ref.at[o] for o in owners]
        got = [jnp.zeros((SUB, LANES), jnp.float32) for _ in owners]
        for k in range(slots // 4):
            rows = [None] * len(owners)
            for j in range(4):
                for t in range(len(owners)):
                    value = tab_ref[pl.ds(at[t][4 * k + j] - 2 * j, SUB), :]
                    rows[t] = value if j == 0 else jnp.where(pair[j], value, rows[t])
            for t in range(len(owners)):
                got[t] = jnp.where(quad == k, jnp.take_along_axis(rows[t], low[t], axis=1), got[t])
        for t, o in enumerate(owners):
            inner = jnp.sum(jnp.where(is_inner, got[t], 0.0), axis=0, keepdims=True)
            outer = jnp.sum(jnp.where(is_outer, got[t], 0.0), axis=0, keepdims=True)
            out_ref[pl.ds(o, 1), :] = inner + frac_ref[pl.ds(o, 1), :] * (outer - inner)

    def body(i, carry):
        team_sizes(TEAM, (i * parts + part) * TEAM, order_ref, count_ref, work)
        return carry

    lax.fori_loop(0, out_ref.shape[0] // (TEAM * parts), body, 0)


def lookup_call(order, counts, idx, tab, low, frac, part, parts, column=None):
    extra = () if column is None else (column,)
    return pl.pallas_call(
        lambda *refs: lookup_kernel(part, parts, column is not None, *refs),
        out_shape=jax.ShapeDtypeStruct(low.shape, jnp.float32),
        in_specs=[SMEM, SMEM] + [ANY] * (4 + len(extra)),
        out_specs=VMEM,
        scratch_shapes=[
            pltpu.SMEM(idx.shape, jnp.int32),
            pltpu.VMEM(tab.shape, jnp.float32),
            pltpu.VMEM(low.shape, jnp.int32),
            pltpu.VMEM(frac.shape, jnp.float32),
            pltpu.SemaphoreType.DMA((4 + len(extra),)),
        ],
        cost_estimate=cost(12, 5 << 20),
        name="lookup",
    )(order, counts, idx, tab, low, frac, *extra)


def scan_kernel(reverse, in_ref, out_ref, *field_ref):
    blocks = in_ref.shape[0] // SUB
    total = jnp.zeros((SUB, LANES), jnp.float32)
    for b in range(blocks - 1, -1, -1) if reverse else range(blocks):
        out_ref[4 * b:4 * b + 2, :] = total[2:4]
        out_ref[4 * b + 2:4 * b + 4, :] = total[6:8]
        total = total + in_ref[SUB * b:SUB * (b + 1), :]
    if field_ref:
        field_ref[0][...] = in_ref[pl.ds(0, field_ref[0].shape[0], stride=FIELDS), :]


def scan_call(parts, devices, reverse, field):
    shapes = [jax.ShapeDtypeStruct((devices * (FIELDS - 2), LANES), jnp.float32)]
    if field:
        shapes.append(jax.ShapeDtypeStruct((devices, LANES), jnp.float32))
    return pl.pallas_call(
        lambda *refs: scan_kernel(reverse, *refs),
        out_shape=shapes,
        cost_estimate=cost(1, 1 << 18),
        compiler_params=pltpu.CompilerParams(vmem_limit_bytes=4 << 20),
        name="scan",
    )(parts)


def exchange(rows, devices):
    parts = rows.reshape(devices, rows.shape[0] // devices, LANES)
    parts = lax.all_to_all(parts, BOTH, split_axis=0, concat_axis=0, tiled=True)
    return parts.reshape(rows.shape)


def halves(x):
    high = x.astype(jnp.bfloat16)
    return high, (x - high.astype(jnp.float32)).astype(jnp.bfloat16)


def star_kernel(devices, count_ref, pix_ref, off_ref, held_ref, col_ref, frac_ref,
                pay_ref, here_ref, inner_ref, acc_ref, tail_ref):
    groups = off_ref.shape[0]
    rows = 2 * SUB
    offt = jnp.transpose(off_ref[...])
    offt = jnp.concatenate(halves(offt), axis=1)
    group_id = lax.broadcasted_iota(jnp.int32, (groups, LANES), 0).astype(jnp.bfloat16)
    lane_id = lax.broadcasted_iota(jnp.int32, (LANES, LANES), 0)
    slot = lax.broadcasted_iota(jnp.int32, (rows, LANES), 1)
    sub = lax.broadcasted_iota(jnp.int32, (rows, LANES), 0)
    one = jnp.ones((groups, LANES), jnp.bfloat16)
    zero = jnp.zeros((groups, LANES), jnp.bfloat16)
    acc_ref[...] = jnp.zeros_like(acc_ref)
    pay_ref[pl.ds(1, devices, stride=FIELDS), :] = jnp.zeros((devices, LANES), jnp.float32)

    def body(b):
        at = pl.ds(pl.multiple_of(b * rows, rows), rows)
        pix = pix_ref[at, :]
        high = lax.shift_right_logical(pix, 7)
        high = (lax.rem(high, devices)) * (groups // devices) + lax.div(high, devices)
        high = high.astype(jnp.float32).astype(jnp.bfloat16)
        low = pix & 127
        pick = jnp.concatenate([jnp.where(group_id == high[j:j + 1, :], one, zero) for j in range(rows)], axis=1)
        found = jnp.dot(offt, jnp.concatenate((pick, pick), axis=0), preferred_element_type=jnp.float32)
        lanes = [lane_id == low[j:j + 1, :] for j in range(rows)]
        off_at = []
        for j in range(rows):
            part = found[:, j * LANES:(j + 1) * LANES]
            part = jnp.where(lanes[j], part, 0.0)
            off_at.append(jnp.sum(part, axis=0, keepdims=True))
        column = col_ref[at, :] + jnp.concatenate(off_at, axis=0)
        obs = held_ref[pl.ds(b * rows * FIELDS, rows, stride=FIELDS), :]
        inv = held_ref[pl.ds(b * rows * FIELDS + 1, rows, stride=FIELDS), :]
        live = jnp.zeros((rows, LANES), jnp.int32)
        for j in range(rows):
            live = jnp.where(sub == j, count_ref[0, b * rows + j], live)
        transmit = jnp.exp(-jnp.where(slot < live, column, 0.0))
        residual = jnp.where(slot < live, (obs - (1.0 - transmit)) * inv, 0.0)
        pull = -residual * inv * transmit
        inner = (1.0 - frac_ref[at, :]) * pull
        pay_ref[pl.ds(b * rows * FIELDS, rows, stride=FIELDS), :] = residual
        here_ref[at, :] = pull - inner
        inner_ref[at, :] = inner
        spread = []
        for j in range(rows):
            spread.append(jnp.concatenate(halves(jnp.where(lanes[j], pull[j:j + 1, :], 0.0)), axis=0))
        spread = jnp.concatenate(spread, axis=1)
        acc_ref[...] += lax.dot_general(
            pick, spread, (((1,), (1,)), ((), ())), preferred_element_type=jnp.float32)

    @pl.loop(0, pix_ref.shape[0] // rows)
    def _(b):
        body(b)

    tail_ref[...] = acc_ref[:, :LANES] + acc_ref[:, LANES:]
    for e in range(groups // devices):
        pay_ref[pl.ds(2 + e, devices, stride=FIELDS), :] = tail_ref[pl.ds(e, devices, stride=groups // devices), :]


def star_call(count, pix, off, held, column, frac, devices):
    slots = jax.ShapeDtypeStruct(pix.shape, jnp.float32)
    return pl.pallas_call(
        lambda *refs: star_kernel(devices, *refs),
        out_shape=[jax.ShapeDtypeStruct(held.shape, jnp.float32), slots, slots],
        in_specs=[SMEM] + [VMEM] * 5,
        out_specs=[VMEM] * 3,
        scratch_shapes=[pltpu.VMEM((off.shape[0], 2 * LANES), jnp.float32), pltpu.VMEM(off.shape, jnp.float32)],
        cost_estimate=cost(8, 1 << 20),
        name="star",
    )(count, pix, off, held, column, frac)


def spread_kernel(order_ref, count_ref, *refs):
    sources, out_hbm, targets = refs[:4], refs[4], refs[5:9]
    accs = refs[9:9 + ACCS]
    sem, in_sem = refs[9 + ACCS:]
    idx_ref, low_ref, here_ref, inner_ref = targets
    started = fetch(sources, targets, in_sem)
    total_rows = out_hbm.shape[0]
    piece = total_rows // SPLIT

    def clear(i, carry):
        for acc in accs:
            acc[pl.ds(pl.multiple_of(i * PACK, PACK), PACK), :] = jnp.zeros((PACK, LANES), jnp.float32)
        return carry

    lax.fori_loop(0, total_rows // PACK, clear, 0)
    for copy in started:
        copy.wait()
    lane = lax.broadcasted_iota(jnp.int32, (SUB, LANES), 1)
    sub = lax.broadcasted_iota(jnp.int32, (SUB, LANES), 0)
    pair = sub >> 1
    in_pair = [pair == j for j in range(4)]
    even = (sub & 1) == 0

    def work(owners, slots):
        def row_of(ref, o):
            return jnp.broadcast_to(ref[pl.ds(o, 1), :], (SUB, LANES))

        low = [row_of(low_ref, o) for o in owners]
        value = [jnp.where(even, row_of(inner_ref, o), row_of(here_ref, o)) for o in owners]
        at = [idx_ref.at[o] for o in owners]
        turn = 0
        for k in range(slots // 4):
            pick = pair + 4 * k
            four = []
            for t in range(len(owners)):
                here = jnp.take_along_axis(low[t], pick, axis=1) == lane
                four.append(jnp.where(here, jnp.take_along_axis(value[t], pick, axis=1), 0.0))
            for j in range(4):
                for t in range(len(owners)):
                    acc = accs[turn % ACCS]
                    turn += 1
                    rows = pl.ds(at[t][4 * k + j] - 2 * j, SUB)
                    acc[rows, :] = acc[rows, :] + jnp.where(in_pair[j], four[t], 0.0)

    def body(i, carry):
        team_sizes(PAIR, i * PAIR, order_ref, count_ref, work)
        return carry

    lax.fori_loop(0, idx_ref.shape[0] // PAIR, body, 0)

    copies = []
    for i in range(SPLIT):
        def gather(k, carry, i=i):
            rows = pl.ds(pl.multiple_of(i * piece + k * PACK, PACK), PACK)
            total = accs[0][rows, :]
            for acc in accs[1:]:
                total = total + acc[rows, :]
            accs[0][rows, :] = total
            return carry

        lax.fori_loop(0, piece // PACK, gather, 0)
        part = pl.ds(i * piece, piece)
        copy = pltpu.make_async_copy(accs[0].at[part, :], out_hbm.at[part, :], sem.at[i])
        copy.start()
        copies.append(copy)
    for copy in copies:
        copy.wait()


def spread_call(order, counts, idx, low, here, inner, rows):
    shape = (rows, LANES)
    return pl.pallas_call(
        spread_kernel,
        out_shape=jax.ShapeDtypeStruct(shape, jnp.float32),
        in_specs=[SMEM, SMEM] + [ANY] * 4,
        out_specs=ANY,
        scratch_shapes=[pltpu.SMEM(idx.shape, jnp.int32), pltpu.VMEM(low.shape, jnp.int32)]
        + [pltpu.VMEM(here.shape, jnp.float32)] * 2
        + [pltpu.VMEM(shape, jnp.float32)] * ACCS
        + [pltpu.SemaphoreType.DMA((SPLIT,)), pltpu.SemaphoreType.DMA((4,))],
        cost_estimate=cost(30, 5 << 20),
        name="spread",
    )(order, counts, idx, low, here, inner)


def chunked(work, inputs, outputs):
    for i in range(CHUNKS):
        for copy in inputs(i):
            copy.start()

    def step(i, carry):
        for copy in inputs(i):
            copy.wait()
        work(i)
        for copy in outputs(i):
            copy.start()
        return carry

    lax.fori_loop(0, CHUNKS, step, 0)
    for i in range(CHUNKS):
        for copy in outputs(i):
            copy.wait()


def extinction_kernel(shells, devices, off_ref, tab_hbm, out_hbm, tab_ref, out_ref, in_sem, out_sem):
    tall = shells + 1
    groups = off_ref.shape[0]
    per = groups // CHUNKS

    def inputs(i):
        rows = pl.ds(LEAD + i * per * tall, per * tall)
        return [pltpu.make_async_copy(tab_hbm.at[rows, :], tab_ref.at[rows, :], in_sem.at[i])]

    def outputs(i):
        rows = pl.ds(i * per * SUB, per * SUB)
        return [pltpu.make_async_copy(out_ref.at[:, rows, :], out_hbm.at[:, rows, :], out_sem.at[i])]

    def work(i):
        for k in range(per):
            g = i * per + k
            off = off_ref[pl.ds((g % devices) * (groups // devices) + g // devices, 1), :]
            for b in range(shells // SUB):
                value = tab_ref[pl.ds(LEAD + g * tall + 1 + b * SUB, SUB), :] + off
                out_ref[b, pl.ds(pl.multiple_of(g * SUB, SUB), SUB), :] = value

    chunked(work, inputs, outputs)


def extinction_call(tab, off, shells, devices):
    shape = (shells // SUB, off.shape[0] * SUB, LANES)
    return pl.pallas_call(
        lambda *refs: extinction_kernel(shells, devices, *refs),
        in_specs=[VMEM, ANY],
        out_specs=ANY,
        out_shape=jax.ShapeDtypeStruct(shape, jnp.float32),
        scratch_shapes=[
            pltpu.VMEM(tab.shape, jnp.float32),
            pltpu.VMEM(shape, jnp.float32),
            pltpu.SemaphoreType.DMA((CHUNKS,)),
            pltpu.SemaphoreType.DMA((CHUNKS,)),
        ],
        cost_estimate=cost(4, 8 << 20),
        name="extinction",
    )(off, tab)


def sensitivity_kernel(shells, devices, off_ref, dens_hbm, drop_hbm, out_hbm, dens_ref, drop_ref, out_ref,
                       in_sem, out_sem):
    tall = shells + 1
    groups = off_ref.shape[0]
    share = groups // devices
    per = groups // CHUNKS

    def inputs(i):
        flat = pl.ds(i * per * shells, per * shells)
        rows = pl.ds(LEAD + i * per * tall, per * tall)
        return [
            pltpu.make_async_copy(dens_hbm.at[flat, :], dens_ref.at[flat, :], in_sem.at[0, i]),
            pltpu.make_async_copy(drop_hbm.at[rows, :], drop_ref.at[rows, :], in_sem.at[1, i]),
        ]

    def outputs(i):
        rows = pl.ds(i * per * SUB, per * SUB)
        return [pltpu.make_async_copy(out_ref.at[:, rows, :], out_hbm.at[:, rows, :], out_sem.at[i])]

    def work(i):
        for k in range(per // SUB):
            g = i * (per // SUB) + k
            first = g * SUB
            total = off_ref[pl.ds((first % devices) * share + first // devices, SUB, stride=share), :]
            for r in range(shells - 1, -1, -1):
                total = total + drop_ref[pl.ds(LEAD + g * SUB * tall + 1 + r, SUB, stride=tall), :]
                out_ref.at[r // SUB][pl.ds(g * SUB * SUB + r % SUB, SUB, stride=SUB), :] = (
                    dens_ref[pl.ds((g * shells + r) * SUB, SUB), :] * total)

    chunked(work, inputs, outputs)


def sensitivity_call(dens, drop, off, shells, devices):
    shape = (shells // SUB, off.shape[0] * SUB, LANES)
    return pl.pallas_call(
        lambda *refs: sensitivity_kernel(shells, devices, *refs),
        in_specs=[VMEM, ANY, ANY],
        out_specs=ANY,
        out_shape=jax.ShapeDtypeStruct(shape, jnp.float32),
        scratch_shapes=[
            pltpu.VMEM(dens.shape, jnp.float32),
            pltpu.VMEM(drop.shape, jnp.float32),
            pltpu.VMEM(shape, jnp.float32),
            pltpu.SemaphoreType.DMA((2, CHUNKS)),
            pltpu.SemaphoreType.DMA((CHUNKS,)),
        ],
        cost_estimate=cost(5, 12 << 20),
        name="sensitivity",
    )(off, dens, drop)


def to_tiles(x):
    shells, pixels = x.shape
    groups = pixels // LANES
    x = x.reshape(shells // SUB, SUB, groups, LANES).transpose(0, 2, 1, 3)
    return x.reshape(shells // SUB, groups * SUB, LANES)


def from_tiles(x):
    bands, rows, lanes = x.shape
    groups = rows // SUB
    x = x.reshape(bands, groups, SUB, lanes).transpose(0, 2, 1, 3)
    return x.reshape(bands * SUB, groups * lanes)


def edge_rows(x, rows):
    count, pixels = rows.stop - rows.start, x.shape[1]
    part = x[rows].reshape(count, pixels // LANES, LANES).transpose(1, 0, 2)
    return part


def sorted_owners(count):
    n = count.shape[0]
    a = lax.broadcasted_iota(jnp.int32, (n, n), 0)
    b = lax.broadcasted_iota(jnp.int32, (n, n), 1)
    ahead = (count[None, :] > count[:, None]) | ((count[None, :] == count[:, None]) & (b < a))
    place = jnp.sum(ahead.astype(jnp.int32), axis=1)
    mine = place[None, :] == a
    return jnp.sum(jnp.where(mine, b, 0), axis=1), jnp.sum(jnp.where(mine, count[None, :], 0), axis=1)


def body(excitation, star_shell, star_pixel, star_fraction, star_count, observed, inverse_error):
    shells, pixels = excitation.shape
    blocks = lax.axis_size("shell")
    devices = blocks * lax.axis_size("sky")
    me = lax.axis_index("shell")
    thickness = depth_span / (shells * blocks)
    groups = pixels // LANES
    tall = shells + 1

    up = [(i, i + 1) for i in range(blocks - 1)]
    down = [(i + 1, i) for i in range(blocks - 1)]
    from_below = lax.ppermute(edge_rows(excitation, slice(shells - PASSES, shells)), "shell", up)
    from_above = lax.ppermute(edge_rows(excitation, slice(0, PASSES)), "shell", down)

    pixel, fraction = star_pixel[0], star_fraction[0]
    low = pixel & (LANES - 1)
    idx = (pixel >> 7) * tall + star_shell[0] + LEAD
    order, counts = sorted_owners(star_count[0])
    from_below, from_above, idx, low, order, counts = lax.optimization_barrier(
        (from_below, from_above, idx, low, order, counts))
    edge = jnp.stack(((me == 0).astype(jnp.float32), (me == blocks - 1).astype(jnp.float32)))
    dens, tab, parts = density_call(
        to_tiles(excitation),
        from_below.reshape(groups * PASSES, LANES),
        from_above.reshape(groups * PASSES, LANES),
        edge, observed[:, 0], inverse_error[:, 0], shells, groups, devices, thickness)

    held = exchange(parts, devices)
    offset = exchange(scan_call(held, devices, False, False)[0], devices)
    column = lookup_call(order, counts, idx, tab, low, fraction, 0, 2)
    column = lookup_call(order, counts, idx, tab, low, fraction, 1, 2, column)

    parts, here, inner = star_call(star_count, pixel, offset, held, column, fraction, devices)
    extinction = extinction_call(tab, offset, shells, devices)
    parts, extinction = lax.optimization_barrier((exchange(parts, devices), extinction))
    sums, residual = scan_call(parts, devices, True, True)
    tail_offset = exchange(sums, devices)

    rows = table_rows(groups, tall)
    drop = spread_call(order, counts, idx, low, here, inner, rows)
    sensitivity = sensitivity_call(dens, drop, tail_offset, shells, devices)
    return from_tiles(extinction), from_tiles(sensitivity), residual[:, None, :]


def solution(mesh):
    placed = (
        P("shell", "sky"),
        P(BOTH, None, None),
        P(BOTH, None, None),
        P(BOTH, None, None),
        P(BOTH, None),
        P(None, BOTH, None),
        P(None, BOTH, None),
    )
    return jax.shard_map(
        body,
        mesh=mesh,
        in_specs=placed,
        out_specs=(P("shell", "sky"), P("shell", "sky"), P(None, BOTH, None)),
        check_vma=False,
    )
```

```python
import math
import jax
import jax.numpy as jnp
from jax import lax
from jax.experimental import pallas as pl
from jax.experimental.pallas import tpu as pltpu
from jax.sharding import PartitionSpec as P

PASSES = 4
LANES = 128
SUB = 8
LEAD = 8
ACCS = 6
TEAM = 4
PAIR = 2
STEP = 16
CHUNKS = 8
SPLIT = 7
PACK = 64
FIELDS = 4
LOG2E = math.log2(math.e)
BOTH = ("shell", "sky")


depth_span = 2.0

VMEM = pl.BlockSpec(memory_space=pltpu.VMEM)
SMEM = pl.BlockSpec(memory_space=pltpu.SMEM)
ANY = pl.BlockSpec(memory_space=pl.ANY)


def cost(micros, nbytes):
    return pl.CostEstimate(flops=int(micros * 2e8), bytes_accessed=int(nbytes), transcendentals=0)


def taps():
    power = [1.0]
    total = [0.0] * (2 * PASSES + 1)
    for k in range(PASSES + 1):
        for i, v in enumerate(power):
            total[PASSES - k + i] += v
        wider = [0.0] * (len(power) + 2)
        for i, v in enumerate(power):
            wider[i] += 0.3 * v
            wider[i + 1] += 0.35 * v
            wider[i + 2] += 0.3 * v
        power = wider
    return total[PASSES:]


def table_rows(groups, tall):
    unit = SPLIT * PACK
    return -(-(LEAD + groups * tall + SUB) // unit) * unit


def density_kernel(shells, groups, devices, thickness, edge_ref, obs_ref, inv_ref, exc_hbm, up_hbm, down_hbm,
                   tab_hbm, pay_ref, exc_ref, up_ref, down_ref, tab_ref, in_sem, out_sem):
    tall = shells + 1
    per = groups // CHUNKS
    weight = [v * LOG2E for v in taps()]
    low_edge = edge_ref[0]
    high_edge = edge_ref[1]

    def inputs(i):
        wide = pl.ds(i * per * SUB, per * SUB)
        thin = pl.ds(i * per * PASSES, per * PASSES)
        return [
            pltpu.make_async_copy(exc_hbm.at[:, wide, :], exc_ref.at[:, wide, :], in_sem.at[0, i]),
            pltpu.make_async_copy(up_hbm.at[thin, :], up_ref.at[thin, :], in_sem.at[1, i]),
            pltpu.make_async_copy(down_hbm.at[thin, :], down_ref.at[thin, :], in_sem.at[2, i]),
        ]

    def outputs(i):
        tall_rows = pl.ds(LEAD + i * per * tall, per * tall)
        return [pltpu.make_async_copy(tab_ref.at[tall_rows, :], tab_hbm.at[tall_rows, :], out_sem.at[i])]

    for i in range(CHUNKS):
        for copy in inputs(i):
            copy.start()
    pay_ref[pl.ds(0, devices, stride=FIELDS), :] = obs_ref[...]
    pay_ref[pl.ds(1, devices, stride=FIELDS), :] = inv_ref[...]

    def group(g):
        exc = {}
        for r in range(shells):
            exc[r] = exc_ref.at[r // SUB][pl.ds(g * SUB * SUB + r % SUB, SUB, stride=SUB), :]
        for k in range(PASSES):
            low = up_ref[pl.ds(g * SUB * PASSES + PASSES - 1 - k, SUB, stride=PASSES), :]
            high = down_ref[pl.ds(g * SUB * PASSES + k, SUB, stride=PASSES), :]
            if k:
                low = low - low_edge * exc[k - 1]
                high = high - high_edge * exc[shells - k]
            exc[-1 - k] = low
            exc[shells + k] = high
        tab_ref[pl.ds(LEAD + g * SUB * tall, SUB, stride=tall), :] = jnp.zeros((SUB, LANES), jnp.float32)
        total = None
        for r in range(shells):
            value = weight[0] * exc[r]
            for k in range(1, PASSES + 1):
                value = value + weight[k] * (exc[r - k] + exc[r + k])
            step = jnp.exp2(value) * thickness
            total = step if total is None else total + step
            tab_ref[pl.ds(LEAD + g * SUB * tall + 1 + r, SUB, stride=tall), :] = total
        first = g * SUB
        pay_ref[pl.ds((first % devices) * FIELDS + 2 + first // devices, SUB, stride=FIELDS), :] = total

    def chunk(i, carry):
        for copy in inputs(i):
            copy.wait()
        for k in range(per // SUB):
            group(i * (per // SUB) + k)
        for copy in outputs(i):
            copy.start()
        return carry

    lax.fori_loop(0, CHUNKS, chunk, 0)
    for i in range(CHUNKS):
        for copy in outputs(i):
            copy.wait()


def density_call(exc, up, down, edge, obs, inv, shells, groups, devices, thickness):
    tall = shells + 1
    rows = table_rows(groups, tall)
    return pl.pallas_call(
        lambda *refs: density_kernel(shells, groups, devices, thickness, *refs),
        in_specs=[SMEM, VMEM, VMEM, ANY, ANY, ANY],
        out_specs=[ANY, VMEM],
        out_shape=[
            jax.ShapeDtypeStruct((rows, LANES), jnp.float32),
            jax.ShapeDtypeStruct((devices * FIELDS, LANES), jnp.float32),
        ],
        scratch_shapes=[
            pltpu.VMEM(exc.shape, jnp.float32),
            pltpu.VMEM(up.shape, jnp.float32),
            pltpu.VMEM(down.shape, jnp.float32),
            pltpu.VMEM((rows, LANES), jnp.float32),
            pltpu.SemaphoreType.DMA((3, CHUNKS)),
            pltpu.SemaphoreType.DMA((CHUNKS,)),
        ],
        cost_estimate=cost(8, 12 << 20),
        name="density",
    )(edge, obs, inv, exc, up, down)


def team_sizes(team, first, order_ref, count_ref, work):
    steps = lax.div(count_ref[first] + (STEP - 1), STEP)
    for size in range(1, LANES // STEP + 1):
        @pl.when(steps == size)
        def _(size=size):
            work([order_ref[first + t] for t in range(team)], size * STEP)


def fetch(sources, targets, sem):
    copies = [pltpu.make_async_copy(x, y, sem.at[i]) for i, (x, y) in enumerate(zip(sources, targets))]
    for copy in copies:
        copy.start()
    return copies


def lookup_kernel(part, parts, chained, order_ref, count_ref, idx_ref, tab_ref, low_ref, frac_ref, *refs):
    out_ref = refs[-1]
    out_ref[...] = refs[0][...] if chained else jnp.zeros_like(out_ref)
    lane = lax.broadcasted_iota(jnp.int32, (SUB, LANES), 1)
    sub = lax.broadcasted_iota(jnp.int32, (SUB, LANES), 0)
    pair = [(sub >> 1) == j for j in range(4)]
    quad = lane >> 2
    is_inner = sub == (lane & 3) * 2
    is_outer = sub == (lane & 3) * 2 + 1

    def work(owners, slots):
        low = [jnp.broadcast_to(low_ref[pl.ds(o, 1), :], (SUB, LANES)) for o in owners]
        at = [idx_ref.at[o] for o in owners]
        got = [jnp.zeros((SUB, LANES), jnp.float32) for _ in owners]
        for k in range(slots // 4):
            rows = [None] * len(owners)
            for j in range(4):
                for t in range(len(owners)):
                    value = tab_ref[pl.ds(at[t][4 * k + j] - 2 * j, SUB), :]
                    rows[t] = value if j == 0 else jnp.where(pair[j], value, rows[t])
            for t in range(len(owners)):
                got[t] = jnp.where(quad == k, jnp.take_along_axis(rows[t], low[t], axis=1), got[t])
        for t, o in enumerate(owners):
            inner = jnp.sum(jnp.where(is_inner, got[t], 0.0), axis=0, keepdims=True)
            outer = jnp.sum(jnp.where(is_outer, got[t], 0.0), axis=0, keepdims=True)
            out_ref[pl.ds(o, 1), :] = inner + frac_ref[pl.ds(o, 1), :] * (outer - inner)

    def body(i, carry):
        team_sizes(TEAM, (i * parts + part) * TEAM, order_ref, count_ref, work)
        return carry

    lax.fori_loop(0, out_ref.shape[0] // (TEAM * parts), body, 0)


def lookup_call(order, counts, idx, tab, low, frac, part, parts, column=None):
    extra = () if column is None else (column,)
    return pl.pallas_call(
        lambda *refs: lookup_kernel(part, parts, column is not None, *refs),
        out_shape=jax.ShapeDtypeStruct(low.shape, jnp.float32),
        in_specs=[SMEM, SMEM, SMEM] + [VMEM] * (3 + len(extra)),
        out_specs=VMEM,
        cost_estimate=cost(12, 5 << 20),
        name="lookup",
    )(order, counts, idx, tab, low, frac, *extra)


def scan_kernel(reverse, in_ref, out_ref, *field_ref):
    blocks = in_ref.shape[0] // SUB
    total = jnp.zeros((SUB, LANES), jnp.float32)
    for b in range(blocks - 1, -1, -1) if reverse else range(blocks):
        out_ref[4 * b:4 * b + 2, :] = total[2:4]
        out_ref[4 * b + 2:4 * b + 4, :] = total[6:8]
        total = total + in_ref[SUB * b:SUB * (b + 1), :]
    if field_ref:
        field_ref[0][...] = in_ref[pl.ds(0, field_ref[0].shape[0], stride=FIELDS), :]


def scan_call(parts, devices, reverse, field):
    shapes = [jax.ShapeDtypeStruct((devices * (FIELDS - 2), LANES), jnp.float32)]
    if field:
        shapes.append(jax.ShapeDtypeStruct((devices, LANES), jnp.float32))
    return pl.pallas_call(
        lambda *refs: scan_kernel(reverse, *refs),
        out_shape=shapes,
        cost_estimate=cost(1, 1 << 18),
        compiler_params=pltpu.CompilerParams(vmem_limit_bytes=4 << 20),
        name="scan",
    )(parts)


def exchange(rows, devices):
    parts = rows.reshape(devices, rows.shape[0] // devices, LANES)
    parts = lax.all_to_all(parts, BOTH, split_axis=0, concat_axis=0, tiled=True)
    return parts.reshape(rows.shape)


def halves(x):
    high = x.astype(jnp.bfloat16)
    return high, (x - high.astype(jnp.float32)).astype(jnp.bfloat16)


def star_kernel(devices, count_ref, pix_ref, off_ref, held_ref, col_ref, frac_ref,
                pay_ref, here_ref, inner_ref, acc_ref, tail_ref):
    groups = off_ref.shape[0]
    rows = 2 * SUB
    offt = jnp.transpose(off_ref[...])
    offt = jnp.concatenate(halves(offt), axis=1)
    group_id = lax.broadcasted_iota(jnp.int32, (groups, LANES), 0).astype(jnp.bfloat16)
    lane_id = lax.broadcasted_iota(jnp.int32, (LANES, LANES), 0)
    slot = lax.broadcasted_iota(jnp.int32, (rows, LANES), 1)
    sub = lax.broadcasted_iota(jnp.int32, (rows, LANES), 0)
    one = jnp.ones((groups, LANES), jnp.bfloat16)
    zero = jnp.zeros((groups, LANES), jnp.bfloat16)
    acc_ref[...] = jnp.zeros_like(acc_ref)
    pay_ref[pl.ds(1, devices, stride=FIELDS), :] = jnp.zeros((devices, LANES), jnp.float32)

    def body(b):
        at = pl.ds(pl.multiple_of(b * rows, rows), rows)
        pix = pix_ref[at, :]
        high = lax.shift_right_logical(pix, 7)
        high = (lax.rem(high, devices)) * (groups // devices) + lax.div(high, devices)
        high = high.astype(jnp.float32).astype(jnp.bfloat16)
        low = pix & 127
        pick = jnp.concatenate([jnp.where(group_id == high[j:j + 1, :], one, zero) for j in range(rows)], axis=1)
        found = jnp.dot(offt, jnp.concatenate((pick, pick), axis=0), preferred_element_type=jnp.float32)
        lanes = [lane_id == low[j:j + 1, :] for j in range(rows)]
        off_at = []
        for j in range(rows):
            part = found[:, j * LANES:(j + 1) * LANES]
            part = jnp.where(lanes[j], part, 0.0)
            off_at.append(jnp.sum(part, axis=0, keepdims=True))
        column = col_ref[at, :] + jnp.concatenate(off_at, axis=0)
        obs = held_ref[pl.ds(b * rows * FIELDS, rows, stride=FIELDS), :]
        inv = held_ref[pl.ds(b * rows * FIELDS + 1, rows, stride=FIELDS), :]
        live = jnp.zeros((rows, LANES), jnp.int32)
        for j in range(rows):
            live = jnp.where(sub == j, count_ref[0, b * rows + j], live)
        transmit = jnp.exp(-jnp.where(slot < live, column, 0.0))
        residual = jnp.where(slot < live, (obs - (1.0 - transmit)) * inv, 0.0)
        pull = -residual * inv * transmit
        inner = (1.0 - frac_ref[at, :]) * pull
        pay_ref[pl.ds(b * rows * FIELDS, rows, stride=FIELDS), :] = residual
        here_ref[at, :] = pull - inner
        inner_ref[at, :] = inner
        spread = []
        for j in range(rows):
            spread.append(jnp.concatenate(halves(jnp.where(lanes[j], pull[j:j + 1, :], 0.0)), axis=0))
        spread = jnp.concatenate(spread, axis=1)
        acc_ref[...] += lax.dot_general(
            pick, spread, (((1,), (1,)), ((), ())), preferred_element_type=jnp.float32)

    @pl.loop(0, pix_ref.shape[0] // rows)
    def _(b):
        body(b)

    tail_ref[...] = acc_ref[:, :LANES] + acc_ref[:, LANES:]
    for e in range(groups // devices):
        pay_ref[pl.ds(2 + e, devices, stride=FIELDS), :] = tail_ref[pl.ds(e, devices, stride=groups // devices), :]


def star_call(count, pix, off, held, column, frac, devices):
    slots = jax.ShapeDtypeStruct(pix.shape, jnp.float32)
    return pl.pallas_call(
        lambda *refs: star_kernel(devices, *refs),
        out_shape=[jax.ShapeDtypeStruct(held.shape, jnp.float32), slots, slots],
        in_specs=[SMEM] + [VMEM] * 5,
        out_specs=[VMEM] * 3,
        scratch_shapes=[pltpu.VMEM((off.shape[0], 2 * LANES), jnp.float32), pltpu.VMEM(off.shape, jnp.float32)],
        cost_estimate=cost(8, 1 << 20),
        name="star",
    )(count, pix, off, held, column, frac)


def spread_kernel(order_ref, count_ref, *refs):
    sources, out_hbm, targets = refs[:4], refs[4], refs[5:9]
    accs = refs[9:9 + ACCS]
    sem, in_sem = refs[9 + ACCS:]
    idx_ref, low_ref, here_ref, inner_ref = targets
    started = fetch(sources, targets, in_sem)
    total_rows = out_hbm.shape[0]
    piece = total_rows // SPLIT

    def clear(i, carry):
        for acc in accs:
            acc[pl.ds(pl.multiple_of(i * PACK, PACK), PACK), :] = jnp.zeros((PACK, LANES), jnp.float32)
        return carry

    lax.fori_loop(0, total_rows // PACK, clear, 0)
    for copy in started:
        copy.wait()
    lane = lax.broadcasted_iota(jnp.int32, (SUB, LANES), 1)
    sub = lax.broadcasted_iota(jnp.int32, (SUB, LANES), 0)
    pair = sub >> 1
    in_pair = [pair == j for j in range(4)]
    even = (sub & 1) == 0

    def work(owners, slots):
        def row_of(ref, o):
            return jnp.broadcast_to(ref[pl.ds(o, 1), :], (SUB, LANES))

        low = [row_of(low_ref, o) for o in owners]
        value = [jnp.where(even, row_of(inner_ref, o), row_of(here_ref, o)) for o in owners]
        at = [idx_ref.at[o] for o in owners]
        turn = 0
        for k in range(slots // 4):
            pick = pair + 4 * k
            four = []
            for t in range(len(owners)):
                here = jnp.take_along_axis(low[t], pick, axis=1) == lane
                four.append(jnp.where(here, jnp.take_along_axis(value[t], pick, axis=1), 0.0))
            for j in range(4):
                for t in range(len(owners)):
                    acc = accs[turn % ACCS]
                    turn += 1
                    rows = pl.ds(at[t][4 * k + j] - 2 * j, SUB)
                    acc[rows, :] = acc[rows, :] + jnp.where(in_pair[j], four[t], 0.0)

    def body(i, carry):
        team_sizes(PAIR, i * PAIR, order_ref, count_ref, work)
        return carry

    lax.fori_loop(0, idx_ref.shape[0] // PAIR, body, 0)

    copies = []
    for i in range(SPLIT):
        def gather(k, carry, i=i):
            rows = pl.ds(pl.multiple_of(i * piece + k * PACK, PACK), PACK)
            total = accs[0][rows, :]
            for acc in accs[1:]:
                total = total + acc[rows, :]
            accs[0][rows, :] = total
            return carry

        lax.fori_loop(0, piece // PACK, gather, 0)
        part = pl.ds(i * piece, piece)
        copy = pltpu.make_async_copy(accs[0].at[part, :], out_hbm.at[part, :], sem.at[i])
        copy.start()
        copies.append(copy)
    for copy in copies:
        copy.wait()


def spread_call(order, counts, idx, low, here, inner, rows):
    shape = (rows, LANES)
    return pl.pallas_call(
        spread_kernel,
        out_shape=jax.ShapeDtypeStruct(shape, jnp.float32),
        in_specs=[SMEM, SMEM] + [ANY] * 4,
        out_specs=ANY,
        scratch_shapes=[pltpu.SMEM(idx.shape, jnp.int32), pltpu.VMEM(low.shape, jnp.int32)]
        + [pltpu.VMEM(here.shape, jnp.float32)] * 2
        + [pltpu.VMEM(shape, jnp.float32)] * ACCS
        + [pltpu.SemaphoreType.DMA((SPLIT,)), pltpu.SemaphoreType.DMA((4,))],
        cost_estimate=cost(30, 5 << 20),
        name="spread",
    )(order, counts, idx, low, here, inner)


def chunked(work, inputs, outputs):
    for i in range(CHUNKS):
        for copy in inputs(i):
            copy.start()

    def step(i, carry):
        for copy in inputs(i):
            copy.wait()
        work(i)
        for copy in outputs(i):
            copy.start()
        return carry

    lax.fori_loop(0, CHUNKS, step, 0)
    for i in range(CHUNKS):
        for copy in outputs(i):
            copy.wait()


def extinction_kernel(shells, devices, off_ref, tab_hbm, out_hbm, tab_ref, out_ref, in_sem, out_sem):
    tall = shells + 1
    groups = off_ref.shape[0]
    per = groups // CHUNKS

    def inputs(i):
        rows = pl.ds(LEAD + i * per * tall, per * tall)
        return [pltpu.make_async_copy(tab_hbm.at[rows, :], tab_ref.at[rows, :], in_sem.at[i])]

    def outputs(i):
        rows = pl.ds(i * per * SUB, per * SUB)
        return [pltpu.make_async_copy(out_ref.at[:, rows, :], out_hbm.at[:, rows, :], out_sem.at[i])]

    def work(i):
        for k in range(per):
            g = i * per + k
            off = off_ref[pl.ds((g % devices) * (groups // devices) + g // devices, 1), :]
            for b in range(shells // SUB):
                value = tab_ref[pl.ds(LEAD + g * tall + 1 + b * SUB, SUB), :] + off
                out_ref[b, pl.ds(pl.multiple_of(g * SUB, SUB), SUB), :] = value

    chunked(work, inputs, outputs)


def extinction_call(tab, off, shells, devices):
    shape = (shells // SUB, off.shape[0] * SUB, LANES)
    return pl.pallas_call(
        lambda *refs: extinction_kernel(shells, devices, *refs),
        in_specs=[VMEM, ANY],
        out_specs=ANY,
        out_shape=jax.ShapeDtypeStruct(shape, jnp.float32),
        scratch_shapes=[
            pltpu.VMEM(tab.shape, jnp.float32),
            pltpu.VMEM(shape, jnp.float32),
            pltpu.SemaphoreType.DMA((CHUNKS,)),
            pltpu.SemaphoreType.DMA((CHUNKS,)),
        ],
        cost_estimate=cost(4, 8 << 20),
        name="extinction",
    )(off, tab)


def sensitivity_kernel(shells, devices, thickness, off_ref, tab_hbm, drop_hbm, out_hbm, tab_ref, drop_ref, out_ref,
                       in_sem, out_sem):
    tall = shells + 1
    groups = off_ref.shape[0]
    share = groups // devices
    per = groups // CHUNKS

    def inputs(i):
        rows = pl.ds(LEAD + i * per * tall, per * tall)
        return [
            pltpu.make_async_copy(tab_hbm.at[rows, :], tab_ref.at[rows, :], in_sem.at[0, i]),
            pltpu.make_async_copy(drop_hbm.at[rows, :], drop_ref.at[rows, :], in_sem.at[1, i]),
        ]

    def outputs(i):
        rows = pl.ds(i * per * SUB, per * SUB)
        return [pltpu.make_async_copy(out_ref.at[:, rows, :], out_hbm.at[:, rows, :], out_sem.at[i])]

    def work(i):
        for k in range(per // SUB):
            g = i * (per // SUB) + k
            first = g * SUB
            total = off_ref[pl.ds((first % devices) * share + first // devices, SUB, stride=share), :]
            scale = 1.0 / thickness
            outer = tab_ref[pl.ds(LEAD + g * SUB * tall + shells, SUB, stride=tall), :]
            for r in range(shells - 1, -1, -1):
                inner = tab_ref[pl.ds(LEAD + g * SUB * tall + r, SUB, stride=tall), :]
                total = total + drop_ref[pl.ds(LEAD + g * SUB * tall + 1 + r, SUB, stride=tall), :]
                out_ref.at[r // SUB][pl.ds(g * SUB * SUB + r % SUB, SUB, stride=SUB), :] = (
                    (outer - inner) * scale * total)
                outer = inner

    chunked(work, inputs, outputs)


def sensitivity_call(tab, drop, off, shells, devices, thickness):
    shape = (shells // SUB, off.shape[0] * SUB, LANES)
    return pl.pallas_call(
        lambda *refs: sensitivity_kernel(shells, devices, thickness, *refs),
        in_specs=[VMEM, ANY, ANY],
        out_specs=ANY,
        out_shape=jax.ShapeDtypeStruct(shape, jnp.float32),
        scratch_shapes=[
            pltpu.VMEM(tab.shape, jnp.float32),
            pltpu.VMEM(drop.shape, jnp.float32),
            pltpu.VMEM(shape, jnp.float32),
            pltpu.SemaphoreType.DMA((2, CHUNKS)),
            pltpu.SemaphoreType.DMA((CHUNKS,)),
        ],
        cost_estimate=cost(5, 12 << 20),
        name="sensitivity",
    )(off, tab, drop)


def to_tiles(x):
    shells, pixels = x.shape
    groups = pixels // LANES
    x = x.reshape(shells // SUB, SUB, groups, LANES).transpose(0, 2, 1, 3)
    return x.reshape(shells // SUB, groups * SUB, LANES)


def from_tiles(x):
    bands, rows, lanes = x.shape
    groups = rows // SUB
    x = x.reshape(bands, groups, SUB, lanes).transpose(0, 2, 1, 3)
    return x.reshape(bands * SUB, groups * lanes)


def edge_rows(x, rows):
    count, pixels = rows.stop - rows.start, x.shape[1]
    part = x[rows].reshape(count, pixels // LANES, LANES).transpose(1, 0, 2)
    return part


def sorted_owners(count):
    n = count.shape[0]
    a = lax.broadcasted_iota(jnp.int32, (n, n), 0)
    b = lax.broadcasted_iota(jnp.int32, (n, n), 1)
    ahead = (count[None, :] > count[:, None]) | ((count[None, :] == count[:, None]) & (b < a))
    place = jnp.sum(ahead.astype(jnp.int32), axis=1)
    mine = place[None, :] == a
    return jnp.sum(jnp.where(mine, b, 0), axis=1), jnp.sum(jnp.where(mine, count[None, :], 0), axis=1)


def body(excitation, star_shell, star_pixel, star_fraction, star_count, observed, inverse_error):
    shells, pixels = excitation.shape
    blocks = lax.axis_size("shell")
    devices = blocks * lax.axis_size("sky")
    me = lax.axis_index("shell")
    thickness = depth_span / (shells * blocks)
    groups = pixels // LANES
    tall = shells + 1

    up = [(i, i + 1) for i in range(blocks - 1)]
    down = [(i + 1, i) for i in range(blocks - 1)]
    from_below = lax.ppermute(edge_rows(excitation, slice(shells - PASSES, shells)), "shell", up)
    from_above = lax.ppermute(edge_rows(excitation, slice(0, PASSES)), "shell", down)

    pixel, fraction = star_pixel[0], star_fraction[0]
    low = pixel & (LANES - 1)
    idx = (pixel >> 7) * tall + star_shell[0] + LEAD
    order, counts = sorted_owners(star_count[0])
    from_below, from_above, idx, low, order, counts = lax.optimization_barrier(
        (from_below, from_above, idx, low, order, counts))
    edge = jnp.stack(((me == 0).astype(jnp.float32), (me == blocks - 1).astype(jnp.float32)))
    tab, parts = density_call(
        to_tiles(excitation),
        from_below.reshape(groups * PASSES, LANES),
        from_above.reshape(groups * PASSES, LANES),
        edge, observed[:, 0], inverse_error[:, 0], shells, groups, devices, thickness)

    held = exchange(parts, devices)
    offset = exchange(scan_call(held, devices, False, False)[0], devices)
    column = lookup_call(order, counts, idx, tab, low, fraction, 0, 2)
    column = lookup_call(order, counts, idx, tab, low, fraction, 1, 2, column)

    parts, here, inner = star_call(star_count, pixel, offset, held, column, fraction, devices)
    extinction = extinction_call(tab, offset, shells, devices)
    parts, extinction = lax.optimization_barrier((exchange(parts, devices), extinction))
    sums, residual = scan_call(parts, devices, True, True)
    tail_offset = exchange(sums, devices)

    rows = table_rows(groups, tall)
    drop = spread_call(order, counts, idx, low, here, inner, rows)
    sensitivity = sensitivity_call(tab, drop, tail_offset, shells, devices, thickness)
    return from_tiles(extinction), from_tiles(sensitivity), residual[:, None, :]


def solution(mesh):
    placed = (
        P("shell", "sky"),
        P(BOTH, None, None),
        P(BOTH, None, None),
        P(BOTH, None, None),
        P(BOTH, None),
        P(None, BOTH, None),
        P(None, BOTH, None),
    )
    return jax.shard_map(
        body,
        mesh=mesh,
        in_specs=placed,
        out_specs=(P("shell", "sky"), P("shell", "sky"), P(None, BOTH, None)),
        check_vma=False,
    )
```

```python
import math
import jax
import jax.numpy as jnp
from jax import lax
from jax.experimental import pallas as pl
from jax.experimental.pallas import tpu as pltpu
from jax.sharding import PartitionSpec as P

PASSES = 4
LANES = 128
SUB = 8
LEAD = 8
ACCS = 6
TEAM = 4
PAIR = 2
STEP = 32
CHUNKS = 8
SPLIT = 7
PACK = 64
FIELDS = 4
LOG2E = math.log2(math.e)
BOTH = ("shell", "sky")


depth_span = 2.0

VMEM = pl.BlockSpec(memory_space=pltpu.VMEM)
SMEM = pl.BlockSpec(memory_space=pltpu.SMEM)
ANY = pl.BlockSpec(memory_space=pl.ANY)


def cost(micros, nbytes):
    return pl.CostEstimate(flops=int(micros * 2e8), bytes_accessed=int(nbytes), transcendentals=0)


def taps():
    power = [1.0]
    total = [0.0] * (2 * PASSES + 1)
    for k in range(PASSES + 1):
        for i, v in enumerate(power):
            total[PASSES - k + i] += v
        wider = [0.0] * (len(power) + 2)
        for i, v in enumerate(power):
            wider[i] += 0.3 * v
            wider[i + 1] += 0.35 * v
            wider[i + 2] += 0.3 * v
        power = wider
    return total[PASSES:]


def table_rows(groups, tall):
    unit = SPLIT * PACK
    return -(-(LEAD + groups * tall + SUB) // unit) * unit


def density_kernel(shells, groups, devices, thickness, edge_ref, obs_ref, inv_ref, exc_hbm, up_hbm, down_hbm,
                   tab_hbm, pay_ref, exc_ref, up_ref, down_ref, tab_ref, in_sem, out_sem):
    tall = shells + 1
    per = groups // CHUNKS
    weight = [v * LOG2E for v in taps()]
    low_edge = edge_ref[0]
    high_edge = edge_ref[1]

    def inputs(i):
        wide = pl.ds(i * per * SUB, per * SUB)
        thin = pl.ds(i * per * PASSES, per * PASSES)
        return [
            pltpu.make_async_copy(exc_hbm.at[:, wide, :], exc_ref.at[:, wide, :], in_sem.at[0, i]),
            pltpu.make_async_copy(up_hbm.at[thin, :], up_ref.at[thin, :], in_sem.at[1, i]),
            pltpu.make_async_copy(down_hbm.at[thin, :], down_ref.at[thin, :], in_sem.at[2, i]),
        ]

    def outputs(i):
        tall_rows = pl.ds(LEAD + i * per * tall, per * tall)
        return [pltpu.make_async_copy(tab_ref.at[tall_rows, :], tab_hbm.at[tall_rows, :], out_sem.at[i])]

    for i in range(CHUNKS):
        for copy in inputs(i):
            copy.start()
    pay_ref[pl.ds(0, devices, stride=FIELDS), :] = obs_ref[...]
    pay_ref[pl.ds(1, devices, stride=FIELDS), :] = inv_ref[...]

    def group(g):
        exc = {}
        for r in range(shells):
            exc[r] = exc_ref.at[r // SUB][pl.ds(g * SUB * SUB + r % SUB, SUB, stride=SUB), :]
        for k in range(PASSES):
            low = up_ref[pl.ds(g * SUB * PASSES + PASSES - 1 - k, SUB, stride=PASSES), :]
            high = down_ref[pl.ds(g * SUB * PASSES + k, SUB, stride=PASSES), :]
            if k:
                low = low - low_edge * exc[k - 1]
                high = high - high_edge * exc[shells - k]
            exc[-1 - k] = low
            exc[shells + k] = high
        tab_ref[pl.ds(LEAD + g * SUB * tall, SUB, stride=tall), :] = jnp.zeros((SUB, LANES), jnp.float32)
        total = None
        for r in range(shells):
            value = weight[0] * exc[r]
            for k in range(1, PASSES + 1):
                value = value + weight[k] * (exc[r - k] + exc[r + k])
            step = jnp.exp2(value) * thickness
            total = step if total is None else total + step
            tab_ref[pl.ds(LEAD + g * SUB * tall + 1 + r, SUB, stride=tall), :] = total
        first = g * SUB
        pay_ref[pl.ds((first % devices) * FIELDS + 2 + first // devices, SUB, stride=FIELDS), :] = total

    def chunk(i, carry):
        for copy in inputs(i):
            copy.wait()
        for k in range(per // SUB):
            group(i * (per // SUB) + k)
        for copy in outputs(i):
            copy.start()
        return carry

    lax.fori_loop(0, CHUNKS, chunk, 0)
    for i in range(CHUNKS):
        for copy in outputs(i):
            copy.wait()


def density_call(exc, up, down, edge, obs, inv, shells, groups, devices, thickness):
    tall = shells + 1
    rows = table_rows(groups, tall)
    return pl.pallas_call(
        lambda *refs: density_kernel(shells, groups, devices, thickness, *refs),
        in_specs=[SMEM, VMEM, VMEM, ANY, ANY, ANY],
        out_specs=[ANY, VMEM],
        out_shape=[
            jax.ShapeDtypeStruct((rows, LANES), jnp.float32),
            jax.ShapeDtypeStruct((devices * FIELDS, LANES), jnp.float32),
        ],
        scratch_shapes=[
            pltpu.VMEM(exc.shape, jnp.float32),
            pltpu.VMEM(up.shape, jnp.float32),
            pltpu.VMEM(down.shape, jnp.float32),
            pltpu.VMEM((rows, LANES), jnp.float32),
            pltpu.SemaphoreType.DMA((3, CHUNKS)),
            pltpu.SemaphoreType.DMA((CHUNKS,)),
        ],
        cost_estimate=cost(8, 12 << 20),
        name="density",
    )(edge, obs, inv, exc, up, down)


def team_sizes(team, first, order_ref, count_ref, work):
    steps = lax.div(count_ref[first] + (STEP - 1), STEP)
    for size in range(1, LANES // STEP + 1):
        @pl.when(steps == size)
        def _(size=size):
            work([order_ref[first + t] for t in range(team)], size * STEP)


def fetch(sources, targets, sem):
    copies = [pltpu.make_async_copy(x, y, sem.at[i]) for i, (x, y) in enumerate(zip(sources, targets))]
    for copy in copies:
        copy.start()
    return copies


def lookup_kernel(part, parts, chained, order_ref, count_ref, idx_ref, tab_ref, low_ref, frac_ref, *refs):
    out_ref = refs[-1]
    out_ref[...] = refs[0][...] if chained else jnp.zeros_like(out_ref)
    lane = lax.broadcasted_iota(jnp.int32, (SUB, LANES), 1)
    sub = lax.broadcasted_iota(jnp.int32, (SUB, LANES), 0)
    pair = [(sub >> 1) == j for j in range(4)]
    quad = lane >> 2
    is_inner = sub == (lane & 3) * 2
    is_outer = sub == (lane & 3) * 2 + 1

    def work(owners, slots):
        low = [jnp.broadcast_to(low_ref[pl.ds(o, 1), :], (SUB, LANES)) for o in owners]
        at = [idx_ref.at[o] for o in owners]
        got = [jnp.zeros((SUB, LANES), jnp.float32) for _ in owners]
        for k in range(slots // 4):
            rows = [None] * len(owners)
            for j in range(4):
                for t in range(len(owners)):
                    value = tab_ref[pl.ds(at[t][4 * k + j] - 2 * j, SUB), :]
                    rows[t] = value if j == 0 else jnp.where(pair[j], value, rows[t])
            for t in range(len(owners)):
                got[t] = jnp.where(quad == k, jnp.take_along_axis(rows[t], low[t], axis=1), got[t])
        for t, o in enumerate(owners):
            inner = jnp.sum(jnp.where(is_inner, got[t], 0.0), axis=0, keepdims=True)
            outer = jnp.sum(jnp.where(is_outer, got[t], 0.0), axis=0, keepdims=True)
            out_ref[pl.ds(o, 1), :] = inner + frac_ref[pl.ds(o, 1), :] * (outer - inner)

    def body(i, carry):
        team_sizes(TEAM, (i * parts + part) * TEAM, order_ref, count_ref, work)
        return carry

    lax.fori_loop(0, out_ref.shape[0] // (TEAM * parts), body, 0)


def lookup_call(order, counts, idx, tab, low, frac, part, parts, column=None):
    extra = () if column is None else (column,)
    return pl.pallas_call(
        lambda *refs: lookup_kernel(part, parts, column is not None, *refs),
        out_shape=jax.ShapeDtypeStruct(low.shape, jnp.float32),
        in_specs=[SMEM, SMEM, SMEM] + [VMEM] * (3 + len(extra)),
        out_specs=VMEM,
        cost_estimate=cost(12, 5 << 20),
        name="lookup",
    )(order, counts, idx, tab, low, frac, *extra)


def scan_kernel(reverse, in_ref, out_ref, *field_ref):
    blocks = in_ref.shape[0] // SUB
    total = jnp.zeros((SUB, LANES), jnp.float32)
    for b in range(blocks - 1, -1, -1) if reverse else range(blocks):
        out_ref[4 * b:4 * b + 2, :] = total[2:4]
        out_ref[4 * b + 2:4 * b + 4, :] = total[6:8]
        total = total + in_ref[SUB * b:SUB * (b + 1), :]
    if field_ref:
        field_ref[0][...] = in_ref[pl.ds(0, field_ref[0].shape[0], stride=FIELDS), :]


def scan_call(parts, devices, reverse, field):
    shapes = [jax.ShapeDtypeStruct((devices * (FIELDS - 2), LANES), jnp.float32)]
    if field:
        shapes.append(jax.ShapeDtypeStruct((devices, LANES), jnp.float32))
    return pl.pallas_call(
        lambda *refs: scan_kernel(reverse, *refs),
        out_shape=shapes,
        cost_estimate=cost(1, 1 << 18),
        compiler_params=pltpu.CompilerParams(vmem_limit_bytes=4 << 20),
        name="scan",
    )(parts)


def exchange(rows, devices):
    parts = rows.reshape(devices, rows.shape[0] // devices, LANES)
    parts = lax.all_to_all(parts, BOTH, split_axis=0, concat_axis=0, tiled=True)
    return parts.reshape(rows.shape)


def halves(x):
    high = x.astype(jnp.bfloat16)
    return high, (x - high.astype(jnp.float32)).astype(jnp.bfloat16)


def star_kernel(devices, count_ref, pix_ref, off_ref, held_ref, col_ref, frac_ref,
                pay_ref, here_ref, inner_ref, acc_ref, tail_ref):
    groups = off_ref.shape[0]
    rows = 2 * SUB
    offt = jnp.transpose(off_ref[...])
    offt = jnp.concatenate(halves(offt), axis=1)
    group_id = lax.broadcasted_iota(jnp.int32, (groups, LANES), 0).astype(jnp.bfloat16)
    lane_id = lax.broadcasted_iota(jnp.int32, (LANES, LANES), 0)
    slot = lax.broadcasted_iota(jnp.int32, (rows, LANES), 1)
    sub = lax.broadcasted_iota(jnp.int32, (rows, LANES), 0)
    one = jnp.ones((groups, LANES), jnp.bfloat16)
    zero = jnp.zeros((groups, LANES), jnp.bfloat16)
    acc_ref[...] = jnp.zeros_like(acc_ref)
    pay_ref[pl.ds(1, devices, stride=FIELDS), :] = jnp.zeros((devices, LANES), jnp.float32)

    def body(b):
        at = pl.ds(pl.multiple_of(b * rows, rows), rows)
        pix = pix_ref[at, :]
        high = lax.shift_right_logical(pix, 7)
        high = (lax.rem(high, devices)) * (groups // devices) + lax.div(high, devices)
        high = high.astype(jnp.float32).astype(jnp.bfloat16)
        low = pix & 127
        pick = jnp.concatenate([jnp.where(group_id == high[j:j + 1, :], one, zero) for j in range(rows)], axis=1)
        found = jnp.dot(offt, jnp.concatenate((pick, pick), axis=0), preferred_element_type=jnp.float32)
        lanes = [lane_id == low[j:j + 1, :] for j in range(rows)]
        off_at = []
        for j in range(rows):
            part = found[:, j * LANES:(j + 1) * LANES]
            part = jnp.where(lanes[j], part, 0.0)
            off_at.append(jnp.sum(part, axis=0, keepdims=True))
        column = col_ref[at, :] + jnp.concatenate(off_at, axis=0)
        obs = held_ref[pl.ds(b * rows * FIELDS, rows, stride=FIELDS), :]
        inv = held_ref[pl.ds(b * rows * FIELDS + 1, rows, stride=FIELDS), :]
        live = jnp.zeros((rows, LANES), jnp.int32)
        for j in range(rows):
            live = jnp.where(sub == j, count_ref[0, b * rows + j], live)
        transmit = jnp.exp(-jnp.where(slot < live, column, 0.0))
        residual = jnp.where(slot < live, (obs - (1.0 - transmit)) * inv, 0.0)
        pull = -residual * inv * transmit
        inner = (1.0 - frac_ref[at, :]) * pull
        pay_ref[pl.ds(b * rows * FIELDS, rows, stride=FIELDS), :] = residual
        here_ref[at, :] = pull - inner
        inner_ref[at, :] = inner
        spread = []
        for j in range(rows):
            spread.append(jnp.concatenate(halves(jnp.where(lanes[j], pull[j:j + 1, :], 0.0)), axis=0))
        spread = jnp.concatenate(spread, axis=1)
        acc_ref[...] += lax.dot_general(
            pick, spread, (((1,), (1,)), ((), ())), preferred_element_type=jnp.float32)

    @pl.loop(0, pix_ref.shape[0] // rows)
    def _(b):
        body(b)

    tail_ref[...] = acc_ref[:, :LANES] + acc_ref[:, LANES:]
    for e in range(groups // devices):
        pay_ref[pl.ds(2 + e, devices, stride=FIELDS), :] = tail_ref[pl.ds(e, devices, stride=groups // devices), :]


def star_call(count, pix, off, held, column, frac, devices):
    slots = jax.ShapeDtypeStruct(pix.shape, jnp.float32)
    return pl.pallas_call(
        lambda *refs: star_kernel(devices, *refs),
        out_shape=[jax.ShapeDtypeStruct(held.shape, jnp.float32), slots, slots],
        in_specs=[SMEM] + [VMEM] * 5,
        out_specs=[VMEM] * 3,
        scratch_shapes=[pltpu.VMEM((off.shape[0], 2 * LANES), jnp.float32), pltpu.VMEM(off.shape, jnp.float32)],
        cost_estimate=cost(8, 1 << 20),
        name="star",
    )(count, pix, off, held, column, frac)


def spread_kernel(order_ref, count_ref, *refs):
    sources, out_hbm, targets = refs[:4], refs[4], refs[5:9]
    accs = refs[9:9 + ACCS]
    sem, in_sem = refs[9 + ACCS:]
    idx_ref, low_ref, here_ref, inner_ref = targets
    started = fetch(sources, targets, in_sem)
    total_rows = out_hbm.shape[0]
    piece = total_rows // SPLIT

    def clear(i, carry):
        for acc in accs:
            acc[pl.ds(pl.multiple_of(i * PACK, PACK), PACK), :] = jnp.zeros((PACK, LANES), jnp.float32)
        return carry

    lax.fori_loop(0, total_rows // PACK, clear, 0)
    for copy in started:
        copy.wait()
    lane = lax.broadcasted_iota(jnp.int32, (SUB, LANES), 1)
    sub = lax.broadcasted_iota(jnp.int32, (SUB, LANES), 0)
    pair = sub >> 1
    in_pair = [pair == j for j in range(4)]
    even = (sub & 1) == 0

    def work(owners, slots):
        def row_of(ref, o):
            return jnp.broadcast_to(ref[pl.ds(o, 1), :], (SUB, LANES))

        low = [row_of(low_ref, o) for o in owners]
        value = [jnp.where(even, row_of(inner_ref, o), row_of(here_ref, o)) for o in owners]
        at = [idx_ref.at[o] for o in owners]
        turn = 0
        for k in range(slots // 4):
            pick = pair + 4 * k
            four = []
            for t in range(len(owners)):
                here = jnp.take_along_axis(low[t], pick, axis=1) == lane
                four.append(jnp.where(here, jnp.take_along_axis(value[t], pick, axis=1), 0.0))
            for j in range(4):
                for t in range(len(owners)):
                    acc = accs[turn % ACCS]
                    turn += 1
                    rows = pl.ds(at[t][4 * k + j] - 2 * j, SUB)
                    acc[rows, :] = acc[rows, :] + jnp.where(in_pair[j], four[t], 0.0)

    def body(i, carry):
        team_sizes(PAIR, i * PAIR, order_ref, count_ref, work)
        return carry

    lax.fori_loop(0, idx_ref.shape[0] // PAIR, body, 0)

    copies = []
    for i in range(SPLIT):
        def gather(k, carry, i=i):
            rows = pl.ds(pl.multiple_of(i * piece + k * PACK, PACK), PACK)
            total = accs[0][rows, :]
            for acc in accs[1:]:
                total = total + acc[rows, :]
            accs[0][rows, :] = total
            return carry

        lax.fori_loop(0, piece // PACK, gather, 0)
        part = pl.ds(i * piece, piece)
        copy = pltpu.make_async_copy(accs[0].at[part, :], out_hbm.at[part, :], sem.at[i])
        copy.start()
        copies.append(copy)
    for copy in copies:
        copy.wait()


def spread_call(order, counts, idx, low, here, inner, rows):
    shape = (rows, LANES)
    return pl.pallas_call(
        spread_kernel,
        out_shape=jax.ShapeDtypeStruct(shape, jnp.float32),
        in_specs=[SMEM, SMEM] + [ANY] * 4,
        out_specs=ANY,
        scratch_shapes=[pltpu.SMEM(idx.shape, jnp.int32), pltpu.VMEM(low.shape, jnp.int32)]
        + [pltpu.VMEM(here.shape, jnp.float32)] * 2
        + [pltpu.VMEM(shape, jnp.float32)] * ACCS
        + [pltpu.SemaphoreType.DMA((SPLIT,)), pltpu.SemaphoreType.DMA((4,))],
        cost_estimate=cost(30, 5 << 20),
        name="spread",
    )(order, counts, idx, low, here, inner)


def chunked(work, inputs, outputs):
    for i in range(CHUNKS):
        for copy in inputs(i):
            copy.start()

    def step(i, carry):
        for copy in inputs(i):
            copy.wait()
        work(i)
        for copy in outputs(i):
            copy.start()
        return carry

    lax.fori_loop(0, CHUNKS, step, 0)
    for i in range(CHUNKS):
        for copy in outputs(i):
            copy.wait()


def extinction_kernel(shells, devices, off_ref, tab_hbm, out_hbm, tab_ref, out_ref, in_sem, out_sem):
    tall = shells + 1
    groups = off_ref.shape[0]
    per = groups // CHUNKS

    def inputs(i):
        rows = pl.ds(LEAD + i * per * tall, per * tall)
        return [pltpu.make_async_copy(tab_hbm.at[rows, :], tab_ref.at[rows, :], in_sem.at[i])]

    def outputs(i):
        rows = pl.ds(i * per * SUB, per * SUB)
        return [pltpu.make_async_copy(out_ref.at[:, rows, :], out_hbm.at[:, rows, :], out_sem.at[i])]

    def work(i):
        for k in range(per):
            g = i * per + k
            off = off_ref[pl.ds((g % devices) * (groups // devices) + g // devices, 1), :]
            for b in range(shells // SUB):
                value = tab_ref[pl.ds(LEAD + g * tall + 1 + b * SUB, SUB), :] + off
                out_ref[b, pl.ds(pl.multiple_of(g * SUB, SUB), SUB), :] = value

    chunked(work, inputs, outputs)


def extinction_call(tab, off, shells, devices):
    shape = (shells // SUB, off.shape[0] * SUB, LANES)
    return pl.pallas_call(
        lambda *refs: extinction_kernel(shells, devices, *refs),
        in_specs=[VMEM, ANY],
        out_specs=ANY,
        out_shape=jax.ShapeDtypeStruct(shape, jnp.float32),
        scratch_shapes=[
            pltpu.VMEM(tab.shape, jnp.float32),
            pltpu.VMEM(shape, jnp.float32),
            pltpu.SemaphoreType.DMA((CHUNKS,)),
            pltpu.SemaphoreType.DMA((CHUNKS,)),
        ],
        cost_estimate=cost(4, 8 << 20),
        name="extinction",
    )(off, tab)


def sensitivity_kernel(shells, devices, thickness, off_ref, tab_hbm, drop_hbm, out_hbm, tab_ref, drop_ref, out_ref,
                       in_sem, out_sem):
    tall = shells + 1
    groups = off_ref.shape[0]
    share = groups // devices
    per = groups // CHUNKS

    def inputs(i):
        rows = pl.ds(LEAD + i * per * tall, per * tall)
        return [
            pltpu.make_async_copy(tab_hbm.at[rows, :], tab_ref.at[rows, :], in_sem.at[0, i]),
            pltpu.make_async_copy(drop_hbm.at[rows, :], drop_ref.at[rows, :], in_sem.at[1, i]),
        ]

    def outputs(i):
        rows = pl.ds(i * per * SUB, per * SUB)
        return [pltpu.make_async_copy(out_ref.at[:, rows, :], out_hbm.at[:, rows, :], out_sem.at[i])]

    def work(i):
        for k in range(per // SUB):
            g = i * (per // SUB) + k
            first = g * SUB
            total = off_ref[pl.ds((first % devices) * share + first // devices, SUB, stride=share), :]
            scale = 1.0 / thickness
            outer = tab_ref[pl.ds(LEAD + g * SUB * tall + shells, SUB, stride=tall), :]
            for r in range(shells - 1, -1, -1):
                inner = tab_ref[pl.ds(LEAD + g * SUB * tall + r, SUB, stride=tall), :]
                total = total + drop_ref[pl.ds(LEAD + g * SUB * tall + 1 + r, SUB, stride=tall), :]
                out_ref.at[r // SUB][pl.ds(g * SUB * SUB + r % SUB, SUB, stride=SUB), :] = (
                    (outer - inner) * scale * total)
                outer = inner

    chunked(work, inputs, outputs)


def sensitivity_call(tab, drop, off, shells, devices, thickness):
    shape = (shells // SUB, off.shape[0] * SUB, LANES)
    return pl.pallas_call(
        lambda *refs: sensitivity_kernel(shells, devices, thickness, *refs),
        in_specs=[VMEM, ANY, ANY],
        out_specs=ANY,
        out_shape=jax.ShapeDtypeStruct(shape, jnp.float32),
        scratch_shapes=[
            pltpu.VMEM(tab.shape, jnp.float32),
            pltpu.VMEM(drop.shape, jnp.float32),
            pltpu.VMEM(shape, jnp.float32),
            pltpu.SemaphoreType.DMA((2, CHUNKS)),
            pltpu.SemaphoreType.DMA((CHUNKS,)),
        ],
        cost_estimate=cost(5, 12 << 20),
        name="sensitivity",
    )(off, tab, drop)


def to_tiles(x):
    shells, pixels = x.shape
    groups = pixels // LANES
    x = x.reshape(shells // SUB, SUB, groups, LANES).transpose(0, 2, 1, 3)
    return x.reshape(shells // SUB, groups * SUB, LANES)


def from_tiles(x):
    bands, rows, lanes = x.shape
    groups = rows // SUB
    x = x.reshape(bands, groups, SUB, lanes).transpose(0, 2, 1, 3)
    return x.reshape(bands * SUB, groups * lanes)


def edge_rows(x, rows):
    count, pixels = rows.stop - rows.start, x.shape[1]
    part = x[rows].reshape(count, pixels // LANES, LANES).transpose(1, 0, 2)
    return part


def sorted_owners(count):
    n = count.shape[0]
    a = lax.broadcasted_iota(jnp.int32, (n, n), 0)
    b = lax.broadcasted_iota(jnp.int32, (n, n), 1)
    ahead = (count[None, :] > count[:, None]) | ((count[None, :] == count[:, None]) & (b < a))
    place = jnp.sum(ahead.astype(jnp.int32), axis=1)
    mine = place[None, :] == a
    return jnp.sum(jnp.where(mine, b, 0), axis=1), jnp.sum(jnp.where(mine, count[None, :], 0), axis=1)


def body(excitation, star_shell, star_pixel, star_fraction, star_count, observed, inverse_error):
    shells, pixels = excitation.shape
    blocks = lax.axis_size("shell")
    devices = blocks * lax.axis_size("sky")
    me = lax.axis_index("shell")
    thickness = depth_span / (shells * blocks)
    groups = pixels // LANES
    tall = shells + 1

    up = [(i, i + 1) for i in range(blocks - 1)]
    down = [(i + 1, i) for i in range(blocks - 1)]
    from_below = lax.ppermute(edge_rows(excitation, slice(shells - PASSES, shells)), "shell", up)
    from_above = lax.ppermute(edge_rows(excitation, slice(0, PASSES)), "shell", down)

    pixel, fraction = star_pixel[0], star_fraction[0]
    low = pixel & (LANES - 1)
    idx = (pixel >> 7) * tall + star_shell[0] + LEAD
    order, counts = sorted_owners(star_count[0])
    from_below, from_above, idx, low, order, counts = lax.optimization_barrier(
        (from_below, from_above, idx, low, order, counts))
    edge = jnp.stack(((me == 0).astype(jnp.float32), (me == blocks - 1).astype(jnp.float32)))
    tab, parts = density_call(
        to_tiles(excitation),
        from_below.reshape(groups * PASSES, LANES),
        from_above.reshape(groups * PASSES, LANES),
        edge, observed[:, 0], inverse_error[:, 0], shells, groups, devices, thickness)

    held = exchange(parts, devices)
    offset = exchange(scan_call(held, devices, False, False)[0], devices)
    column = lookup_call(order, counts, idx, tab, low, fraction, 0, 2)
    column = lookup_call(order, counts, idx, tab, low, fraction, 1, 2, column)

    parts, here, inner = star_call(star_count, pixel, offset, held, column, fraction, devices)
    extinction = extinction_call(tab, offset, shells, devices)
    parts, extinction = lax.optimization_barrier((exchange(parts, devices), extinction))
    sums, residual = scan_call(parts, devices, True, True)
    tail_offset = exchange(sums, devices)

    rows = table_rows(groups, tall)
    drop = spread_call(order, counts, idx, low, here, inner, rows)
    sensitivity = sensitivity_call(tab, drop, tail_offset, shells, devices, thickness)
    return from_tiles(extinction), from_tiles(sensitivity), residual[:, None, :]


def solution(mesh):
    placed = (
        P("shell", "sky"),
        P(BOTH, None, None),
        P(BOTH, None, None),
        P(BOTH, None, None),
        P(BOTH, None),
        P(None, BOTH, None),
        P(None, BOTH, None),
    )
    return jax.shard_map(
        body,
        mesh=mesh,
        in_specs=placed,
        out_specs=(P("shell", "sky"), P("shell", "sky"), P(None, BOTH, None)),
        check_vma=False,
    )
```
